512 devices in a mesh: stream: 128 (over y, z, core), vert: 4 (over x).
Axes of the slice: x: 4, y: 8, z: 8, core: 2. Of those that a mesh axis runs over, the one named last changes fastest.
Arguments:
- particles: float32 [4096, 4, 7, 128], P('stream', 'vert'), may hold values from -4 to 4, as said below
- phase_flags: int32 [4096, 4, 128], P('stream', 'vert'), may hold values 0 or 1
- neighbours: int32 [4096, 4, 4], P('stream', 'vert'), may hold values from 0 to 7, as said below
- history: bfloat16 [4096, 4, 3, 126, 128], P('stream', 'vert'), may hold values from -160 to 160
- basis_start: float32 [128, 64], replicated, may hold values from -0.5 to 0.5
Outputs:
- new_state: float32 [4096, 4, 7, 128], P('stream', 'vert')
- filtered: float32 [4096, 4, 3, 128], P('stream', 'vert')
The draws below stay inside these ranges and needn't reach their ends.
Inputs may be any that keep to these rules, and one draw needn't show every extreme that they name: `particles`: rows 0 to 2 of a particle lie in 0 to 2, rows 3 to 5 in -4 to 4, row 6 in 0.97 to 1.03. `neighbours`: the 4 codes of one block are distinct.
All inputs are finite; a program needn't handle non-finite values. No bound on the sum of `phase_flags` on one device may be relied on, other than what follows from the above.
Results may differ from the reference program's by a relative error of at most 0.0003.
Values sent between devices are 32-bit elements; how exact they have to be, the bound alone decides.
A program may use at most 64 MiB of HBM per device.

```python
import math
import jax
import jax.numpy as jnp
from jax import lax

PART = 128
NBR = 4
SNAP = 128
RANK = 64
POD_ITERS = 4
GS = 4096
GV = 4
HIST = 126


def velocity_field(key):
    velocity = jnp.clip(jax.random.normal(key, (GS, GV, 3, PART), jnp.float32), -3.9, 3.9)
    return velocity


def draw_particles(key, part):
    key_place = jax.random.fold_in(key, 0)
    key_density = jax.random.fold_in(key, 2)
    position = jax.random.uniform(key_place, (GS, GV, 3, PART), jnp.float32, 0.0, 2.0)
    velocity = velocity_field(jax.random.fold_in(key, 11))
    relative = jax.random.uniform(key_density, (GS, GV, 1, PART), jnp.float32, 0.97, 1.03)
    return jnp.concatenate([position, velocity, relative], axis=2)


def draw_neighbours(key, part):
    scores = jax.random.randint(key, (GS, GV, 8), 0, 1 << 20) * 8 + jnp.arange(8, dtype=jnp.int32)
    order = jnp.argsort(scores, axis=-1, stable=True)
    return order[:, :, :NBR].astype(jnp.int32)


def draw_history(key, part):
    key_column, key_value, key_share = jax.random.split(jax.random.fold_in(key, 29), 3)
    column_scale = jnp.exp(jax.random.uniform(key_column, (HIST,), jnp.float32, 0.0, math.log(10.0)))
    share = jax.random.uniform(key_share, (HIST,), jnp.float32, 0.4, 1.0)
    rising = 1.0 + 2.0 * jnp.arange(GS, dtype=jnp.float32) / max(GS - 1, 1)
    velocity = velocity_field(jax.random.fold_in(key, 11))
    noise = jnp.clip(jax.random.normal(key_value, (GS, GV, 3, HIST, PART), jnp.float32), -5.0, 5.0)
    values = 0.8 * share[:, None] * velocity[:, :, :, None, :] + 0.3 * noise
    return (values * column_scale[:, None] * rising[:, None, None, None, None]).astype(jnp.bfloat16)


def with_ends(entries, rng, smallest, high):
    place = [jax.random.randint(jax.random.fold_in(rng, axis), (), 0, length) for axis, length in enumerate(entries.shape)]
    widest = entries.shape.index(max(entries.shape))
    neighbour = place[:widest] + [(place[widest] + 1) % entries.shape[widest]] + place[widest + 1:]
    return entries.at[tuple(place)].set(smallest).at[tuple(neighbour)].set(high)


def centred(stream_key, extent, width, bound, kind=jnp.bfloat16):
    values = width * jax.random.normal(stream_key, extent, jnp.float32)
    return jnp.clip(values, min=-bound, max=bound).astype(kind)


def setup_inputs(seed: int = 0) -> dict:
    splits = jax.random.split(jax.random.key(seed), 6)
    particles = draw_particles(jax.random.fold_in(splits[5], 71), 0)
    phase_flags = with_ends((jax.random.randint(splits[1], (GS, GV, PART), 0, 4) < 1).astype(jnp.int32), jax.random.fold_in(splits[1], 1), 0, 1)
    neighbours = draw_neighbours(jax.random.fold_in(splits[5], 71), 0)
    history = draw_history(jax.random.fold_in(splits[5], 71), 0)
    basis_start = centred(splits[4], (SNAP, RANK), SNAP ** -0.5, 0.5, jnp.float32)
    return dict(particles=particles, phase_flags=phase_flags, neighbours=neighbours, history=history, basis_start=basis_start)


ALPHA_KERNEL = 21.0 / (16.0 * math.pi)
VOLUME = 1.0 / 16.0
STIFFNESS = 100.0 / 7.0
TIME_STEP = 0.02
GRAVITY = 1.0
SEDIMENT_EXTRA = 1.65

def forces(own_block, near_blocks, cell_shifts):
    separation = own_block[:, None, 0:3, :, None] - near_blocks[:, :, 0:3, None, :] - cell_shifts[:, :, :, None, None]
    radius = jnp.sqrt(lax.optimization_barrier(jnp.sum(separation * separation, axis=2)))
    kernel_reach = jnp.maximum(1.0 - 0.5 * radius, 0.0)
    kernel_slope = -5.0 * ALPHA_KERNEL * kernel_reach ** 3 * near_blocks[:, :, 6, None, :]
    closing = own_block[:, None, 3:6, :, None] - near_blocks[:, :, 3:6, None, :]
    density_rate = lax.optimization_barrier(jnp.sum(kernel_slope * lax.optimization_barrier(jnp.sum(closing * separation, axis=2)), axis=(1, 3)))
    pressure_term = kernel_slope * (own_block[:, None, 7, :, None] + near_blocks[:, :, 7, None, :])
    acceleration = -lax.optimization_barrier(jnp.sum(pressure_term[:, :, None] * separation, axis=(1, 4)))
    return (acceleration, density_rate)

def block_layout(neighbours):
    blocks_stream, blocks_vert = (neighbours.shape[0], neighbours.shape[1])
    offset_code = neighbours + (neighbours >= 4).astype(jnp.int32)
    zero_codes = jnp.zeros((blocks_stream, blocks_vert, 1), jnp.int32)
    stream_step = jnp.concatenate([zero_codes, offset_code // 3 - 1], axis=-1)
    vert_step = jnp.concatenate([zero_codes, offset_code % 3 - 1], axis=-1)
    stream_place = jnp.arange(blocks_stream, dtype=jnp.int32)[:, None, None]
    vert_place = jnp.arange(blocks_vert, dtype=jnp.int32)[None, :, None]
    near_index = (stream_place + 1 + stream_step) * (blocks_vert + 2) + (vert_place + 1 + vert_step)
    list_width = near_index.shape[2]
    cell_shifts = jnp.stack([2.0 * stream_step.astype(jnp.float32), jnp.zeros(stream_step.shape, jnp.float32), 2.0 * vert_step.astype(jnp.float32)], axis=-1)
    return (near_index.reshape(-1, list_width).astype(jnp.int32), cell_shifts.reshape(-1, list_width, 3))

def make_payload(particles, rest_density, particle_mass):
    relative = particles[:, :, 6]
    pressure = STIFFNESS * (relative ** 7 - 1.0) / (rest_density * relative * relative)
    return jnp.concatenate([particles[:, :, 0:6], particle_mass[:, :, None], pressure[:, :, None]], axis=2)

def interact(payload, extended, near_index, cell_shifts, group_limit):
    block_count = payload.shape[0] * payload.shape[1]
    group_size = math.gcd(block_count, group_limit)
    flat_blocks = extended.reshape(-1, 8, payload.shape[3])
    list_width = near_index.shape[1]

    def one_group(pieces):
        own_block, index_part, shift_part = pieces
        near_blocks = jnp.take(flat_blocks, index_part, axis=0)
        return forces(own_block, near_blocks, shift_part)
    acceleration, density_rate = lax.map(one_group, (payload.reshape(block_count // group_size, group_size, 8, -1), near_index.reshape(-1, group_size, list_width), cell_shifts.reshape(-1, group_size, list_width, 3)))
    return (acceleration.reshape(payload.shape[0], payload.shape[1], 3, -1), density_rate.reshape(payload.shape[0], payload.shape[1], -1))

def update(particles, rest_density, acceleration, density_rate):
    gravity_vector = jnp.array([0.0, 0.0, -GRAVITY], jnp.float32)[:, None]
    velocity = particles[:, :, 3:6] + TIME_STEP * (acceleration + gravity_vector)
    position = particles[:, :, 0:3] + TIME_STEP * velocity
    relative = particles[:, :, 6] + TIME_STEP * density_rate / rest_density
    return jnp.concatenate([position, velocity, relative[:, :, None]], axis=2)

def orthonormal(matrix):
    for repeat in range(2):
        inner_product = jnp.dot(matrix.T, matrix, precision=lax.Precision.HIGHEST)
        factor = jnp.linalg.cholesky(inner_product)
        matrix = lax.linalg.triangular_solve(factor, matrix, left_side=False, lower=True, transpose_a=True)
    return matrix

def pod_weights(gram_matrix, basis_start):
    basis_now = orthonormal(basis_start)
    for iteration in range(POD_ITERS):
        basis_now = orthonormal(jnp.dot(gram_matrix, basis_now, precision=lax.Precision.HIGHEST))
    return jnp.dot(basis_now, basis_now[-1], precision=lax.Precision.HIGHEST)

def advance_whole(particles, rest_density, particle_mass, near_index, cell_shifts):
    payload = make_payload(particles, rest_density, particle_mass)
    extended = jnp.pad(payload, ((1, 1), (1, 1), (0, 0), (0, 0)))
    acceleration, density_rate = interact(payload, extended, near_index, cell_shifts, 32)
    return update(particles, rest_density, acceleration, density_rate)

def reference(particles, phase_flags, neighbours, history, basis_start):
    rest_density = 1.0 + SEDIMENT_EXTRA * phase_flags.astype(jnp.float32)
    particle_mass = rest_density * VOLUME
    near_index, cell_shifts = block_layout(neighbours)
    first_state = advance_whole(particles, rest_density, particle_mass, near_index, cell_shifts)
    second_state = advance_whole(first_state, rest_density, particle_mass, near_index, cell_shifts)
    new_snapshots = jnp.stack([first_state[:, :, 3:6], second_state[:, :, 3:6]], axis=3).astype(jnp.bfloat16)
    block_count = particles.shape[0] * particles.shape[1]
    group_size = math.gcd(block_count, 64)
    hist_count = history.shape[3]
    part_count = history.shape[4]
    snap_count = basis_start.shape[0]
    hist_groups = history.reshape(block_count // group_size, group_size, 3, hist_count, part_count)
    new_groups = new_snapshots.reshape(block_count // group_size, group_size, 3, 2, part_count)

    def add_gram(total, pieces):
        snapshots = jnp.concatenate([pieces[0], pieces[1]], axis=2).astype(jnp.float32)
        return (total + jnp.einsum('bcsp,bctp->st', snapshots, snapshots, precision=lax.Precision.HIGHEST), None)
    gram_matrix, unused = lax.scan(add_gram, jnp.zeros((snap_count, snap_count), jnp.float32), (hist_groups, new_groups))
    weights = pod_weights(gram_matrix, basis_start)

    def filter_group(pieces):
        snapshots = jnp.concatenate([pieces[0], pieces[1]], axis=2).astype(jnp.float32)
        return jnp.einsum('bcsp,s->bcp', snapshots, weights, precision=lax.Precision.HIGHEST)
    filtered = lax.map(filter_group, (hist_groups, new_groups)).reshape(particles.shape[0], particles.shape[1], 3, part_count)
    return (second_state, filtered)
```

```python
import functools
import math

import jax
import jax.numpy as jnp
from jax import lax
from jax.experimental import pallas as pl
from jax.experimental.pallas import tpu as pltpu
from jax.sharding import PartitionSpec as P

POD_ITERS = 4
VOLUME = 1.0 / 16.0
STIFFNESS = 100.0 / 7.0
SLOPE = -5.0 * 21.0 / (16.0 * math.pi)
DT = 0.02
SEDIMENT_EXTRA = 1.65

HI = lax.Precision.HIGHEST
NT = (((1,), (1,)), ((), ()))
NN = (((1,), (0,)), ((), ()))
TN = (((0,), (0,)), ((), ()))
BF = jnp.bfloat16
F32 = jnp.float32
MESH = pl.DeviceIdType.MESH
VM = pl.BlockSpec(memory_space=pltpu.VMEM)

def split3(x):
    a = x.astype(BF).astype(F32)
    b = (x - a).astype(BF).astype(F32)
    return a, b, x - a - b


def forces_kernel(codes_ref, ext_ref, relative_ref, out_ref, next_ref):
    blocks = relative_ref.shape[0]
    part = relative_ref.shape[-1]
    row = lax.broadcasted_iota(jnp.int32, (8, part), 0)

    def centred(vert, stream, ds, dv):
        field = ext_ref[vert, stream]
        shift = jnp.where(row == 0, 2.0 * ds - 1.0, jnp.where(row == 1, -1.0, jnp.where(row == 2, 2.0 * dv - 1.0, 0.0)))
        return field + shift

    def norm(half):
        square = half * half
        return square[0:1] + square[1:2] + square[2:3]

    def one_block(b, carry):
        own = centred(1, b + 1, 0.0, 0.0)
        half = 0.5 * own
        target = jnp.where(row < 3, half, jnp.where(row == 3, 1.0, jnp.where(row == 4, norm(half), 0.0)))
        h, m, l = split3(target)
        target = jnp.concatenate([h, h, m, h, l, m], axis=0).astype(BF)
        sums = jnp.zeros((16, part), F32)
        for n in range(5):
            if n == 0:
                vert, stream, ds, dv = 1, b + 1, 0.0, 0.0
            else:
                code = codes_ref[b, n - 1]
                code = jnp.where(code >= 4, code + 1, code)
                third = lax.div(code, 3)
                ds, dv = third - 1, code - 3 * third - 1
                vert, stream = dv + 1, b + 1 + ds
                ds, dv = ds.astype(F32), dv.astype(F32)
            near = centred(vert, stream, ds, dv)
            half = 0.5 * near
            source = jnp.where(row < 3, -2.0 * half, jnp.where(row == 3, norm(half), jnp.where(row == 4, 1.0, 0.0)))
            h, m, l = split3(source)
            source = jnp.concatenate([h, m, h, l, h, m], axis=0).astype(BF)
            mass = near[6:7]
            weighted = jnp.where(row == 6, 1.0, near) * mass
            dots = near[0:3] * near[3:6]
            dot = mass * (dots[0:1] + dots[1:2] + dots[2:3])
            second = jnp.where(row < 3, weighted * near[7:8], jnp.where(row == 3, dot, 0.0))
            fields = jnp.concatenate([weighted, second], axis=0)
            high = fields.astype(BF)
            low = (fields - high.astype(F32)).astype(BF)
            quarter = lax.dot_general(target, source, TN, preferred_element_type=F32)
            quarter = jnp.maximum(quarter, 1e-30)
            reach = jnp.maximum(1.0 - quarter * lax.rsqrt(quarter), 0.0)
            cube = reach * reach * reach
            cube_high = cube.astype(BF)
            cube_low = (cube - cube_high.astype(F32)).astype(BF)
            part_a = lax.dot_general(jnp.concatenate([high, low], axis=0), cube_high, NT, preferred_element_type=F32)
            part_b = lax.dot_general(high, cube_low, NT, preferred_element_type=F32)
            sums = sums + (part_a[0:16] + part_a[16:32] + part_b)
        relative = relative_ref[b]
        density = 16.0 * own[6:7]
        place, speed, pressure = own[0:3], own[3:6], own[7:8]
        total, pressure_total, vx = sums[6:7], sums[7:8], sums[11:12]
        dots = speed * (place * total - sums[0:3]) - place * sums[3:6]
        rate = SLOPE * (dots[0:1] + dots[1:2] + dots[2:3] + vx)
        acc = -SLOPE * (pressure * (place * total - sums[0:3]) + place * pressure_total - sums[8:11])
        gravity = jnp.where(row[0:3] == 2, -1.0, 0.0)
        speed = speed + DT * (acc + gravity)
        place = ext_ref[1, b + 1][0:3] + DT * speed
        relative = relative + DT * rate / density
        power = relative * relative
        power = power * power * power * relative
        pressure = STIFFNESS * (power - 1.0) / (density * relative * relative)
        out_ref[b] = jnp.concatenate([place, speed, relative], axis=0)
        next_ref[b] = jnp.concatenate([place, speed, own[6:7], pressure], axis=0)
        return carry

    lax.fori_loop(0, blocks, one_block, 0)


def forces_step(codes, ext, relative):
    blocks, _, part = relative.shape
    vm = pl.BlockSpec(memory_space=pltpu.VMEM)
    return pl.pallas_call(
        forces_kernel,
        out_shape=(jax.ShapeDtypeStruct((blocks, 7, part), F32), jax.ShapeDtypeStruct((blocks, 8, part), F32)),
        in_specs=[pl.BlockSpec(memory_space=pltpu.SMEM), vm, vm],
        out_specs=(vm, vm),
        name="forces",
    )(codes, ext, relative)

def orthonormal_rows(t):
    rank, width = t.shape
    zero = jnp.zeros((width - rank, width), jnp.float32)
    lane = lax.broadcasted_iota(jnp.int32, (rank, width), 1)
    row = lax.broadcasted_iota(jnp.int32, (rank, width), 0)
    unit = jnp.where(lane == row + rank, 1.0, 0.0)
    work = lax.dot_general(t, jnp.concatenate([t, zero], axis=0), NT, precision=HI) + unit
    eight = lax.broadcasted_iota(jnp.int32, (8, width), 0)
    count = rank // 8

    def panel(p, groups):
        groups = list(groups)
        cols = [
            [jnp.where(g + p < count, jnp.broadcast_to(groups[g][:, c:c + 1], (8, width)), 0.0) for g in range(count)]
            for c in range(8)
        ]
        for k in range(8):
            inv = lax.rsqrt(jnp.broadcast_to(cols[k][0][k:k + 1], (8, width)))
            low = [cols[k][g] * inv for g in range(count)]
            pivot_row = jnp.broadcast_to(groups[0][k:k + 1], (8, width)) * inv
            for c in range(k + 1, 8):
                factor = jnp.broadcast_to(low[0][c:c + 1], (8, width))
                for g in range(count):
                    cols[c][g] = cols[c][g] - low[g] * factor
            groups[0] = jnp.where(eight == k, pivot_row, jnp.where(eight > k, groups[0] - low[0] * pivot_row, groups[0]))
            for g in range(1, count):
                groups[g] = groups[g] - low[g] * pivot_row
        groups = groups[1:] + groups[:1]
        return tuple(pltpu.roll(x, width - 8, 1) for x in groups)

    groups = lax.fori_loop(0, count, panel, tuple(work[8 * g:8 * g + 8] for g in range(count)))
    done = jnp.concatenate(groups, axis=0)
    return lax.dot_general(done, jnp.concatenate([t, zero], axis=0), NN, precision=HI)
def pod_kernel(iters, gram_ref, start_ref, out_ref):
    def half(i, t):
        t = orthonormal_rows(t)
        again = jnp.logical_and(i % 2 == 1, i < 2 * iters + 1)
        return lax.cond(
            again,
            lambda t: lax.dot_general(t, gram_ref[...], NN, precision=HI),
            lambda t: t,
            t,
        )

    t = lax.fori_loop(0, 2 * iters + 2, half, start_ref[...])
    last = jnp.broadcast_to(t[:, -1:], t.shape)
    out_ref[...] = jnp.broadcast_to(jnp.sum(t * last, axis=0, keepdims=True), out_ref.shape)


def pod_weights(gram, start_t, iters=POD_ITERS):
    return pl.pallas_call(
        functools.partial(pod_kernel, iters),
        out_shape=jax.ShapeDtypeStruct((8, gram.shape[0]), jnp.float32),
        in_specs=[pl.BlockSpec(memory_space=pltpu.VMEM)] * 2,
        out_specs=pl.BlockSpec(memory_space=pltpu.VMEM),
        name="pod",
    )(gram, start_t)

SIDES = [(ds, dv) for dv in (-1, 0, 1) for ds in (-1, 0, 1) if (ds, dv) != (0, 0)]


def halo_kernel(own_ref, ext_ref, local_sem, send_sem, recv_sem):
    blocks = own_ref.shape[0]
    streams, verts = lax.axis_size("stream"), lax.axis_size("vert")
    me_s, me_v = lax.axis_index("stream"), lax.axis_index("vert")

    def present(ds, dv):
        s, v = me_s + ds, me_v + dv
        return jnp.logical_and(jnp.logical_and(s >= 0, s < streams), jnp.logical_and(v >= 0, v < verts))

    def rows(ds, start):
        if ds == 0:
            return pl.ds(start, blocks)
        return None

    def copy(index):
        ds, dv = SIDES[index]
        if ds == 0:
            source, target = own_ref, ext_ref.at[1 - dv, pl.ds(1, blocks)]
        elif ds == 1:
            source, target = own_ref.at[pl.ds(blocks - 1, 1)], ext_ref.at[1 - dv, pl.ds(0, 1)]
        else:
            source, target = own_ref.at[pl.ds(0, 1)], ext_ref.at[1 - dv, pl.ds(blocks + 1, 1)]
        return pltpu.make_async_remote_copy(
            src_ref=source,
            dst_ref=target,
            send_sem=send_sem.at[index],
            recv_sem=recv_sem.at[index],
            device_id=(me_s + ds, me_v + dv),
            device_id_type=MESH,
        )

    local = pltpu.make_async_copy(own_ref, ext_ref.at[1, pl.ds(1, blocks)], local_sem)
    local.start()
    barrier = pltpu.get_barrier_semaphore()
    count = 0
    for ds, dv in SIDES:
        here = present(ds, dv)
        count = count + here.astype(jnp.int32)

        @pl.when(here)
        def _():
            pl.semaphore_signal(barrier, inc=1, device_id=(me_s + ds, me_v + dv), device_id_type=MESH)

    pl.semaphore_wait(barrier, count)
    for index, (ds, dv) in enumerate(SIDES):

        @pl.when(present(ds, dv))
        def _():
            copy(index).start()

        @pl.when(jnp.logical_not(present(ds, dv)))
        def _():
            if ds == 0:
                ext_ref[1 + dv, 1 : blocks + 1] = jnp.zeros(own_ref.shape, F32)
            else:
                ext_ref[1 + dv, 0 if ds < 0 else blocks + 1] = jnp.zeros(own_ref.shape[1:], F32)

    for index, (ds, dv) in enumerate(SIDES):
        back = SIDES.index((-ds, -dv))

        @pl.when(present(ds, dv))
        def _():
            copy(index).wait_send()
            copy(back).wait_recv()

    local.wait()


def halo(payload, collective_id):
    blocks, fields, part = payload.shape
    return pl.pallas_call(
        halo_kernel,
        out_shape=jax.ShapeDtypeStruct((3, blocks + 2, fields, part), F32),
        in_specs=[VM],
        out_specs=VM,
        scratch_shapes=[
            pltpu.SemaphoreType.DMA,
            pltpu.SemaphoreType.DMA((8,)),
            pltpu.SemaphoreType.DMA((8,)),
        ],
        compiler_params=pltpu.CompilerParams(collective_id=collective_id, has_side_effects=True),
        name="halo",
    )(payload)


LONG = 8


def reduce_kernel(gram_ref, out_ref, slots, sums, send_sem, recv_sem):
    stream, vert = lax.axis_index("stream"), lax.axis_index("vert")
    core, z, y = stream % 2, (stream // 2) % LONG, stream // (2 * LONG)
    near = vert * 2 + core
    size = gram_ref.shape[0] // LONG

    def near_device(r):
        return (stream - core + r % 2, r // 2)

    def z_device(r):
        return (stream + (r - z) * 2, vert)

    def y_device(r):
        return (stream + (r - y) * 2 * LONG, vert)

    barrier = pltpu.get_barrier_semaphore()
    for me, device in ((near, near_device), (z, z_device), (y, y_device)):
        for step in range(1, LONG):
            pl.semaphore_signal(barrier, inc=1, device_id=device((me + step) % LONG), device_id_type=MESH)
    pl.semaphore_wait(barrier, 3 * (LONG - 1))

    def exchange(stage, me, device, source, target):
        def copy(step):
            other = (me + step) % LONG
            return pltpu.make_async_remote_copy(
                src_ref=source(other),
                dst_ref=target(step),
                send_sem=send_sem.at[stage, step],
                recv_sem=recv_sem.at[stage, step],
                device_id=device(other),
                device_id_type=MESH,
            )

        for step in range(1, LONG):
            copy(step).start()
        for step in range(1, LONG):
            copy(step).wait()

    def total(stage, own):
        for step in range(1, LONG):
            own = own + slots[stage, step]
        return own

    mine = pl.ds(pl.multiple_of(near * size, size), size)
    exchange(
        0, near, near_device,
        lambda other: gram_ref.at[pl.ds(pl.multiple_of(other * size, size), size)],
        lambda step: slots.at[0, step],
    )
    sums[0] = total(0, gram_ref[mine])
    exchange(1, z, z_device, lambda other: sums.at[0], lambda step: slots.at[1, step])
    sums[1] = total(1, sums[0])
    exchange(2, y, y_device, lambda other: sums.at[1], lambda step: slots.at[2, step])
    sums[2] = total(2, sums[1])
    out_ref[mine] = sums[2]
    exchange(3, near, near_device, lambda other: sums.at[2], lambda step: out_ref.at[mine])


def reduce_gram(gram, collective_id):
    size = gram.shape[0] // LONG
    return pl.pallas_call(
        reduce_kernel,
        out_shape=jax.ShapeDtypeStruct(gram.shape, F32),
        in_specs=[VM],
        out_specs=VM,
        scratch_shapes=[
            pltpu.VMEM((3, LONG, size, gram.shape[1]), F32),
            pltpu.VMEM((3, size, gram.shape[1]), F32),
            pltpu.SemaphoreType.DMA((4, LONG)),
            pltpu.SemaphoreType.DMA((4, LONG)),
        ],
        compiler_params=pltpu.CompilerParams(collective_id=collective_id, has_side_effects=True),
        name="reduce",
    )(gram)


def body(particles, phase_flags, neighbours, history, basis_start):
    state = particles[:, 0]
    codes = neighbours[:, 0]
    rest_density = 1.0 + SEDIMENT_EXTRA * phase_flags.astype(F32)
    mass = rest_density * VOLUME
    relative = state[:, 6:7]
    pressure = STIFFNESS * (relative**7 - 1.0) / (rest_density * relative * relative)
    payload = jnp.concatenate([state[:, 0:6], mass, pressure], axis=1)
    first, payload = forces_step(codes, halo(payload, 0), relative)
    second, _ = forces_step(codes, halo(payload, 1), first[:, 6:7])
    newest = jnp.stack([first[:, 3:6], second[:, 3:6]], axis=2).astype(BF)
    snapshots = jnp.concatenate([history[:, 0], newest], axis=2)
    gram = jnp.einsum("acsp,actp->st", snapshots, snapshots, preferred_element_type=F32)
    weights = pod_weights(reduce_gram(gram, 2), basis_start.T)[0]
    filtered = jnp.einsum("acsp,s->acp", snapshots.astype(F32), weights, precision=HI)
    return (second[:, None], filtered[:, None])


def solution(mesh):
    in_specs = (
        P("stream", "vert", None, None),
        P("stream", "vert", None),
        P("stream", "vert", None),
        P("stream", "vert", None, None, None),
        P(),
    )
    out_specs = (P("stream", "vert", None, None), P("stream", "vert", None, None))
    return jax.shard_map(body, mesh=mesh, in_specs=in_specs, out_specs=out_specs, check_vma=False)
```

```python
import functools
import math

import jax
import jax.numpy as jnp
from jax import lax
from jax.experimental import pallas as pl
from jax.experimental.pallas import tpu as pltpu
from jax.sharding import PartitionSpec as P

POD_ITERS = 4
VOLUME = 1.0 / 16.0
STIFFNESS = 100.0 / 7.0
SLOPE = -5.0 * 21.0 / (16.0 * math.pi)
DT = 0.02
SEDIMENT_EXTRA = 1.65

HI = lax.Precision.HIGHEST
NT = (((1,), (1,)), ((), ()))
NN = (((1,), (0,)), ((), ()))
TN = (((0,), (0,)), ((), ()))
BF = jnp.bfloat16
F32 = jnp.float32
MESH = pl.DeviceIdType.MESH
VM = pl.BlockSpec(memory_space=pltpu.VMEM)

def split3(x):
    a = x.astype(BF).astype(F32)
    b = (x - a).astype(BF).astype(F32)
    return a, b, x - a - b


def forces_kernel(codes_ref, ext_ref, relative_ref, out_ref, next_ref):
    blocks = relative_ref.shape[0]
    part = relative_ref.shape[-1]
    row = lax.broadcasted_iota(jnp.int32, (8, part), 0)

    def centred(vert, stream, ds, dv):
        field = ext_ref[vert, stream]
        shift = jnp.where(row == 0, 2.0 * ds - 1.0, jnp.where(row == 1, -1.0, jnp.where(row == 2, 2.0 * dv - 1.0, 0.0)))
        return field + shift

    def norm(half):
        square = half * half
        return square[0:1] + square[1:2] + square[2:3]

    def one_block(b, carry):
        own = centred(1, b + 1, 0.0, 0.0)
        half = 0.5 * own
        target = jnp.where(row < 3, half, jnp.where(row == 3, 1.0, jnp.where(row == 4, norm(half), 0.0)))
        h, m, l = split3(target)
        target = jnp.concatenate([h, h, m, h, l, m], axis=0).astype(BF)
        lefts, rights = [], []
        for n in range(5):
            if n == 0:
                vert, stream, ds, dv = 1, b + 1, 0.0, 0.0
            else:
                code = codes_ref[b, n - 1]
                code = jnp.where(code >= 4, code + 1, code)
                third = lax.div(code, 3)
                ds, dv = third - 1, code - 3 * third - 1
                vert, stream = dv + 1, b + 1 + ds
                ds, dv = ds.astype(F32), dv.astype(F32)
            near = centred(vert, stream, ds, dv)
            half = 0.5 * near
            source = jnp.where(row < 3, -2.0 * half, jnp.where(row == 3, norm(half), jnp.where(row == 4, 1.0, 0.0)))
            h, m, l = split3(source)
            source = jnp.concatenate([h, m, h, l, h, m], axis=0).astype(BF)
            mass = near[6:7]
            weighted = jnp.where(row == 6, 1.0, near) * mass
            dots = near[0:3] * near[3:6]
            dot = mass * (dots[0:1] + dots[1:2] + dots[2:3])
            second = jnp.where(row < 3, weighted * near[7:8], jnp.where(row == 3, dot, 0.0))
            fields = jnp.concatenate([weighted, second], axis=0)
            high = fields.astype(BF)
            low = (fields - high.astype(F32)).astype(BF)
            quarter = lax.dot_general(target, source, TN, preferred_element_type=F32)
            quarter = jnp.maximum(quarter, 1e-30)
            reach = jnp.maximum(1.0 - quarter * lax.rsqrt(quarter), 0.0)
            cube = reach * reach * reach
            cube_high = cube.astype(BF)
            cube_low = (cube - cube_high.astype(F32)).astype(BF)
            left = jnp.concatenate([cube_high, cube_low], axis=1)
            right = jnp.concatenate([jnp.concatenate([high, high], axis=1), jnp.concatenate([low, jnp.zeros_like(low)], axis=1)], axis=0)
            lefts.append(left)
            rights.append(right)
        sums = lax.dot_general(jnp.concatenate(lefts, axis=1), jnp.concatenate(rights, axis=1), NT, preferred_element_type=F32)
        sums = jnp.transpose(sums)
        sums = sums[0:16] + sums[16:32]
        relative = relative_ref[b]
        density = 16.0 * own[6:7]
        place, speed, pressure = own[0:3], own[3:6], own[7:8]
        total, pressure_total, vx = sums[6:7], sums[7:8], sums[11:12]
        dots = speed * (place * total - sums[0:3]) - place * sums[3:6]
        rate = SLOPE * (dots[0:1] + dots[1:2] + dots[2:3] + vx)
        acc = -SLOPE * (pressure * (place * total - sums[0:3]) + place * pressure_total - sums[8:11])
        gravity = jnp.where(row[0:3] == 2, -1.0, 0.0)
        speed = speed + DT * (acc + gravity)
        place = ext_ref[1, b + 1][0:3] + DT * speed
        relative = relative + DT * rate / density
        power = relative * relative
        power = power * power * power * relative
        pressure = STIFFNESS * (power - 1.0) / (density * relative * relative)
        out_ref[b] = jnp.concatenate([place, speed, relative], axis=0)
        next_ref[b] = jnp.concatenate([place, speed, own[6:7], pressure], axis=0)
        return carry

    def several(i, carry):
        for k in range(4):
            one_block(4 * i + k, carry)
        return carry

    lax.fori_loop(0, blocks // 4, several, 0)


def forces_step(codes, ext, relative):
    blocks, _, part = relative.shape
    vm = pl.BlockSpec(memory_space=pltpu.VMEM)
    return pl.pallas_call(
        forces_kernel,
        out_shape=(jax.ShapeDtypeStruct((blocks, 7, part), F32), jax.ShapeDtypeStruct((blocks, 8, part), F32)),
        in_specs=[pl.BlockSpec(memory_space=pltpu.SMEM), vm, vm],
        out_specs=(vm, vm),
        name="forces",
    )(codes, ext, relative)

def orthonormal_rows(t):
    rank, width = t.shape
    zero = jnp.zeros((width - rank, width), jnp.float32)
    lane = lax.broadcasted_iota(jnp.int32, (rank, width), 1)
    row = lax.broadcasted_iota(jnp.int32, (rank, width), 0)
    unit = jnp.where(lane == row + rank, 1.0, 0.0)
    work = lax.dot_general(t, jnp.concatenate([t, zero], axis=0), NT, precision=HI) + unit
    eight = lax.broadcasted_iota(jnp.int32, (8, width), 0)
    count = rank // 8

    def panel(p, groups):
        groups = list(groups)
        cols = [
            [jnp.where(g + p < count, jnp.broadcast_to(groups[g][:, c:c + 1], (8, width)), 0.0) for g in range(count)]
            for c in range(8)
        ]
        for k in range(8):
            inv = lax.rsqrt(jnp.broadcast_to(cols[k][0][k:k + 1], (8, width)))
            low = [cols[k][g] * inv for g in range(count)]
            pivot_row = jnp.broadcast_to(groups[0][k:k + 1], (8, width)) * inv
            for c in range(k + 1, 8):
                factor = jnp.broadcast_to(low[0][c:c + 1], (8, width))
                for g in range(count):
                    cols[c][g] = cols[c][g] - low[g] * factor
            groups[0] = jnp.where(eight == k, pivot_row, jnp.where(eight > k, groups[0] - low[0] * pivot_row, groups[0]))
            for g in range(1, count):
                groups[g] = groups[g] - low[g] * pivot_row
        groups = groups[1:] + groups[:1]
        return tuple(pltpu.roll(x, width - 8, 1) for x in groups)

    groups = lax.fori_loop(0, count, panel, tuple(work[8 * g:8 * g + 8] for g in range(count)))
    done = jnp.concatenate(groups, axis=0)
    return lax.dot_general(done, jnp.concatenate([t, zero], axis=0), NN, precision=HI)
def pod_kernel(iters, gram_ref, start_ref, out_ref):
    def half(i, t):
        t = orthonormal_rows(t)
        again = jnp.logical_and(i % 2 == 1, i < 2 * iters + 1)
        return lax.cond(
            again,
            lambda t: lax.dot_general(t, gram_ref[...], NN, precision=HI),
            lambda t: t,
            t,
        )

    t = lax.fori_loop(0, 2 * iters + 2, half, start_ref[...])
    last = jnp.broadcast_to(t[:, -1:], t.shape)
    out_ref[...] = jnp.broadcast_to(jnp.sum(t * last, axis=0, keepdims=True), out_ref.shape)


def pod_weights(gram, start_t, iters=POD_ITERS):
    return pl.pallas_call(
        functools.partial(pod_kernel, iters),
        out_shape=jax.ShapeDtypeStruct((8, gram.shape[0]), jnp.float32),
        in_specs=[pl.BlockSpec(memory_space=pltpu.VMEM)] * 2,
        out_specs=pl.BlockSpec(memory_space=pltpu.VMEM),
        name="pod",
    )(gram, start_t)

SIDES = [(ds, dv) for dv in (-1, 0, 1) for ds in (-1, 0, 1) if (ds, dv) != (0, 0)]


def halo_kernel(own_ref, ext_ref, local_sem, send_sem, recv_sem):
    blocks = own_ref.shape[0]
    streams, verts = lax.axis_size("stream"), lax.axis_size("vert")
    me_s, me_v = lax.axis_index("stream"), lax.axis_index("vert")

    def present(ds, dv):
        s, v = me_s + ds, me_v + dv
        return jnp.logical_and(jnp.logical_and(s >= 0, s < streams), jnp.logical_and(v >= 0, v < verts))

    def rows(ds, start):
        if ds == 0:
            return pl.ds(start, blocks)
        return None

    def copy(index):
        ds, dv = SIDES[index]
        if ds == 0:
            source, target = own_ref, ext_ref.at[1 - dv, pl.ds(1, blocks)]
        elif ds == 1:
            source, target = own_ref.at[pl.ds(blocks - 1, 1)], ext_ref.at[1 - dv, pl.ds(0, 1)]
        else:
            source, target = own_ref.at[pl.ds(0, 1)], ext_ref.at[1 - dv, pl.ds(blocks + 1, 1)]
        return pltpu.make_async_remote_copy(
            src_ref=source,
            dst_ref=target,
            send_sem=send_sem.at[index],
            recv_sem=recv_sem.at[index],
            device_id=(me_s + ds, me_v + dv),
            device_id_type=MESH,
        )

    local = pltpu.make_async_copy(own_ref, ext_ref.at[1, pl.ds(1, blocks)], local_sem)
    local.start()
    barrier = pltpu.get_barrier_semaphore()
    count = 0
    for ds, dv in SIDES:
        here = present(ds, dv)
        count = count + here.astype(jnp.int32)

        @pl.when(here)
        def _():
            pl.semaphore_signal(barrier, inc=1, device_id=(me_s + ds, me_v + dv), device_id_type=MESH)

    pl.semaphore_wait(barrier, count)
    for index, (ds, dv) in enumerate(SIDES):

        @pl.when(present(ds, dv))
        def _():
            copy(index).start()

        @pl.when(jnp.logical_not(present(ds, dv)))
        def _():
            if ds == 0:
                ext_ref[1 + dv, 1 : blocks + 1] = jnp.zeros(own_ref.shape, F32)
            else:
                ext_ref[1 + dv, 0 if ds < 0 else blocks + 1] = jnp.zeros(own_ref.shape[1:], F32)

    for index, (ds, dv) in enumerate(SIDES):
        back = SIDES.index((-ds, -dv))

        @pl.when(present(ds, dv))
        def _():
            copy(index).wait_send()
            copy(back).wait_recv()

    local.wait()


def halo(payload, collective_id):
    blocks, fields, part = payload.shape
    return pl.pallas_call(
        halo_kernel,
        out_shape=jax.ShapeDtypeStruct((3, blocks + 2, fields, part), F32),
        in_specs=[VM],
        out_specs=VM,
        scratch_shapes=[
            pltpu.SemaphoreType.DMA,
            pltpu.SemaphoreType.DMA((8,)),
            pltpu.SemaphoreType.DMA((8,)),
        ],
        compiler_params=pltpu.CompilerParams(collective_id=collective_id, has_side_effects=True),
        name="halo",
    )(payload)


LONG = 8


def reduce_kernel(gram_ref, out_ref, slots, sums, send_sem, recv_sem):
    stream, vert = lax.axis_index("stream"), lax.axis_index("vert")
    core, z, y = stream % 2, (stream // 2) % LONG, stream // (2 * LONG)
    near = vert * 2 + core
    size = gram_ref.shape[0] // LONG

    def near_device(r):
        return (stream - core + r % 2, r // 2)

    def z_device(r):
        return (stream + (r - z) * 2, vert)

    def y_device(r):
        return (stream + (r - y) * 2 * LONG, vert)

    barrier = pltpu.get_barrier_semaphore()
    for me, device in ((near, near_device), (z, z_device), (y, y_device)):
        for step in range(1, LONG):
            pl.semaphore_signal(barrier, inc=1, device_id=device((me + step) % LONG), device_id_type=MESH)
    pl.semaphore_wait(barrier, 3 * (LONG - 1))

    def exchange(stage, me, device, source, target):
        def copy(step):
            other = (me + step) % LONG
            return pltpu.make_async_remote_copy(
                src_ref=source(other),
                dst_ref=target(step),
                send_sem=send_sem.at[stage, step],
                recv_sem=recv_sem.at[stage, step],
                device_id=device(other),
                device_id_type=MESH,
            )

        for step in range(1, LONG):
            copy(step).start()
        for step in range(1, LONG):
            copy(step).wait()

    def total(stage, own):
        for step in range(1, LONG):
            own = own + slots[stage, step]
        return own

    mine = pl.ds(pl.multiple_of(near * size, size), size)
    exchange(
        0, near, near_device,
        lambda other: gram_ref.at[pl.ds(pl.multiple_of(other * size, size), size)],
        lambda step: slots.at[0, step],
    )
    sums[0] = total(0, gram_ref[mine])
    exchange(1, z, z_device, lambda other: sums.at[0], lambda step: slots.at[1, step])
    sums[1] = total(1, sums[0])
    exchange(2, y, y_device, lambda other: sums.at[1], lambda step: slots.at[2, step])
    sums[2] = total(2, sums[1])
    out_ref[mine] = sums[2]
    exchange(3, near, near_device, lambda other: sums.at[2], lambda step: out_ref.at[mine])


def reduce_gram(gram, collective_id):
    size = gram.shape[0] // LONG
    return pl.pallas_call(
        reduce_kernel,
        out_shape=jax.ShapeDtypeStruct(gram.shape, F32),
        in_specs=[VM],
        out_specs=VM,
        scratch_shapes=[
            pltpu.VMEM((3, LONG, size, gram.shape[1]), F32),
            pltpu.VMEM((3, size, gram.shape[1]), F32),
            pltpu.SemaphoreType.DMA((4, LONG)),
            pltpu.SemaphoreType.DMA((4, LONG)),
        ],
        compiler_params=pltpu.CompilerParams(collective_id=collective_id, has_side_effects=True),
        name="reduce",
    )(gram)


def body(particles, phase_flags, neighbours, history, basis_start):
    state = particles[:, 0]
    codes = neighbours[:, 0]
    rest_density = 1.0 + SEDIMENT_EXTRA * phase_flags.astype(F32)
    mass = rest_density * VOLUME
    relative = state[:, 6:7]
    pressure = STIFFNESS * (relative**7 - 1.0) / (rest_density * relative * relative)
    payload = jnp.concatenate([state[:, 0:6], mass, pressure], axis=1)
    first, payload = forces_step(codes, halo(payload, 0), relative)
    second, _ = forces_step(codes, halo(payload, 1), first[:, 6:7])
    newest = jnp.stack([first[:, 3:6], second[:, 3:6]], axis=2).astype(BF)
    snapshots = jnp.concatenate([history[:, 0], newest], axis=2)
    gram = jnp.einsum("acsp,actp->st", snapshots, snapshots, preferred_element_type=F32)
    weights = pod_weights(reduce_gram(gram, 2), basis_start.T)[0]
    filtered = jnp.einsum("acsp,s->acp", snapshots.astype(F32), weights, precision=HI)
    return (second[:, None], filtered[:, None])


def solution(mesh):
    in_specs = (
        P("stream", "vert", None, None),
        P("stream", "vert", None),
        P("stream", "vert", None),
        P("stream", "vert", None, None, None),
        P(),
    )
    out_specs = (P("stream", "vert", None, None), P("stream", "vert", None, None))
    return jax.shard_map(body, mesh=mesh, in_specs=in_specs, out_specs=out_specs, check_vma=False)
```

```python
import functools
import math

import jax
import jax.numpy as jnp
from jax import lax
from jax.experimental import pallas as pl
from jax.experimental.pallas import tpu as pltpu
from jax.sharding import PartitionSpec as P

POD_ITERS = 4
VOLUME = 1.0 / 16.0
STIFFNESS = 100.0 / 7.0
SLOPE = -5.0 * 21.0 / (16.0 * math.pi)
DT = 0.02
SEDIMENT_EXTRA = 1.65

HI = lax.Precision.HIGHEST
NT = (((1,), (1,)), ((), ()))
NN = (((1,), (0,)), ((), ()))
TN = (((0,), (0,)), ((), ()))
BF = jnp.bfloat16
F32 = jnp.float32
MESH = pl.DeviceIdType.MESH
VM = pl.BlockSpec(memory_space=pltpu.VMEM)

TRIP = 8


def pressure_of(relative, density):
    power = relative * relative
    power = power * power * power * relative
    return STIFFNESS * (power - 1.0) / (density * relative * relative)


def prepare_kernel(state_ref, flags_ref, out_ref):
    blocks = flags_ref.shape[0]
    for field in range(6):
        out_ref[pl.ds(field, blocks, stride=8)] = state_ref[pl.ds(field, blocks, stride=7)]
    density = 1.0 + SEDIMENT_EXTRA * flags_ref[...].astype(F32)
    out_ref[pl.ds(6, blocks, stride=8)] = density * VOLUME
    out_ref[pl.ds(7, blocks, stride=8)] = pressure_of(state_ref[pl.ds(6, blocks, stride=7)], density)


def prepare(state, flags):
    blocks, part = flags.shape
    return pl.pallas_call(
        prepare_kernel,
        out_shape=jax.ShapeDtypeStruct((8 * blocks, part), F32),
        in_specs=[VM, VM],
        out_specs=VM,
        name="prepare",
    )(state, flags).reshape(blocks, 8, part)


def split3(x):
    a = x.astype(BF).astype(F32)
    b = (x - a).astype(BF).astype(F32)
    return a, b, x - a - b


def forces_kernel(codes_ref, ext_ref, state_ref, out_ref, speed_ref, *next_ref):
    blocks, part = ext_ref.shape[1] - 2, ext_ref.shape[3]
    row = lax.broadcasted_iota(jnp.int32, (8, part), 0)

    def centred(vert, stream, ds, dv):
        field = ext_ref[vert, stream]
        shift = jnp.where(row == 0, 2.0 * ds - 1.0, jnp.where(row == 1, -1.0, jnp.where(row == 2, 2.0 * dv - 1.0, 0.0)))
        return field + shift

    def norm(half):
        square = half * half
        return square[0:1] + square[1:2] + square[2:3]

    def one_block(b):
        own = centred(1, b + 1, 0.0, 0.0)
        half = 0.5 * own
        target = jnp.where(row < 3, half, jnp.where(row == 3, 1.0, jnp.where(row == 4, norm(half), 0.0)))
        h, m, l = split3(target)
        target = jnp.concatenate([h, h, m, h, l, m], axis=0).astype(BF)
        lefts, rights = [], []
        for n in range(5):
            if n == 0:
                vert, stream, ds, dv = 1, b + 1, 0.0, 0.0
            else:
                code = codes_ref[n - 1, b]
                code = jnp.where(code >= 4, code + 1, code)
                third = lax.div(code, 3)
                ds, dv = third - 1, code - 3 * third - 1
                vert, stream = dv + 1, b + 1 + ds
                ds, dv = ds.astype(F32), dv.astype(F32)
            near = centred(vert, stream, ds, dv)
            half = 0.5 * near
            source = jnp.where(row < 3, -2.0 * half, jnp.where(row == 3, norm(half), jnp.where(row == 4, 1.0, 0.0)))
            h, m, l = split3(source)
            source = jnp.concatenate([h, m, h, l, h, m], axis=0).astype(BF)
            mass = near[6:7]
            weighted = jnp.where(row == 6, 1.0, near) * mass
            dots = near[0:3] * near[3:6]
            dot = mass * (dots[0:1] + dots[1:2] + dots[2:3])
            second = jnp.where(row < 3, weighted * near[7:8], jnp.where(row == 3, dot, 0.0))
            fields = jnp.concatenate([weighted, second], axis=0)
            high = fields.astype(BF)
            low = (fields - high.astype(F32)).astype(BF)
            quarter = lax.dot_general(target, source, TN, preferred_element_type=F32)
            quarter = jnp.maximum(quarter, 1e-30)
            reach = jnp.maximum(1.0 - quarter * lax.rsqrt(quarter), 0.0)
            cube = reach * reach * reach
            cube_high = cube.astype(BF)
            cube_low = (cube - cube_high.astype(F32)).astype(BF)
            left = jnp.concatenate([cube_high, cube_low], axis=1)
            right = jnp.concatenate([jnp.concatenate([high, high], axis=1), jnp.concatenate([low, jnp.zeros_like(low)], axis=1)], axis=0)
            lefts.append(left)
            rights.append(right)
        sums = lax.dot_general(jnp.concatenate(lefts, axis=1), jnp.concatenate(rights, axis=1), NT, preferred_element_type=F32)
        sums = jnp.transpose(sums)
        sums = sums[0:16] + sums[16:32]
        relative = state_ref[pl.ds(7 * b + 6, 1)]
        density = 16.0 * own[6:7]
        place, speed, pressure = own[0:3], own[3:6], own[7:8]
        total, pressure_total, vx = sums[6:7], sums[7:8], sums[11:12]
        dots = speed * (place * total - sums[0:3]) - place * sums[3:6]
        rate = SLOPE * (dots[0:1] + dots[1:2] + dots[2:3] + vx)
        acc = -SLOPE * (pressure * (place * total - sums[0:3]) + place * pressure_total - sums[8:11])
        gravity = jnp.where(row[0:3] == 2, -1.0, 0.0)
        speed = speed + DT * (acc + gravity)
        place = ext_ref[1, b + 1][0:3] + DT * speed
        relative = relative + DT * rate / density
        out_ref[pl.ds(7 * b, 7)] = jnp.concatenate([place, speed, relative], axis=0)
        for c in range(3):
            speed_ref[c, pl.ds(b, 1)] = speed[c : c + 1]
        if next_ref:
            pressure = pressure_of(relative, density)
            next_ref[0][b] = jnp.concatenate([place, speed, own[6:7], pressure], axis=0)

    def several(i, carry):
        for k in range(TRIP):
            one_block(TRIP * i + k)
        return carry

    lax.fori_loop(0, blocks // TRIP, several, 0)


def forces_step(codes, ext, state, last):
    blocks, part = ext.shape[1] - 2, ext.shape[3]
    shapes = [jax.ShapeDtypeStruct(state.shape, F32), jax.ShapeDtypeStruct((3, blocks, part), F32)]
    if not last:
        shapes.append(jax.ShapeDtypeStruct((blocks, 8, part), F32))
    return pl.pallas_call(
        forces_kernel,
        out_shape=shapes,
        in_specs=[pl.BlockSpec(memory_space=pltpu.SMEM), VM, VM],
        out_specs=[VM] * len(shapes),
        name="forces",
    )(codes, ext, state)


def orthonormal_rows(t):
    rank, width = t.shape
    zero = jnp.zeros((width - rank, width), jnp.float32)
    lane = lax.broadcasted_iota(jnp.int32, (rank, width), 1)
    row = lax.broadcasted_iota(jnp.int32, (rank, width), 0)
    unit = jnp.where(lane == row + rank, 1.0, 0.0)
    work = lax.dot_general(t, jnp.concatenate([t, zero], axis=0), NT, precision=HI) + unit
    eight = lax.broadcasted_iota(jnp.int32, (8, width), 0)
    count = rank // 8

    groups = [work[8 * g:8 * g + 8] for g in range(count)]
    for p in range(count):
        live = range(p, count)
        cols = [{g: jnp.broadcast_to(groups[g][:, 8 * p + c:8 * p + c + 1], (8, width)) for g in live} for c in range(8)]
        for k in range(8):
            inv = lax.rsqrt(jnp.broadcast_to(cols[k][p][k:k + 1], (8, width)))
            low = {g: cols[k][g] * inv for g in live}
            pivot_row = jnp.broadcast_to(groups[p][k:k + 1], (8, width)) * inv
            for c in range(k + 1, 8):
                factor = jnp.broadcast_to(low[p][c:c + 1], (8, width))
                for g in live:
                    cols[c][g] = cols[c][g] - low[g] * factor
            groups[p] = jnp.where(eight == k, pivot_row, jnp.where(eight > k, groups[p] - low[p] * pivot_row, groups[p]))
            for g in range(p + 1, count):
                groups[g] = groups[g] - low[g] * pivot_row
    done = jnp.concatenate(groups, axis=0)
    return lax.dot_general(done, jnp.concatenate([zero, t], axis=0), NN, precision=HI)
def pod_kernel(iters, gram_ref, rows_ref, basis_ref, out_ref, full_ref):
    width = gram_ref.shape[0]
    rows = rows_ref[...]
    across = jnp.transpose(jnp.concatenate([rows, jnp.zeros((width - rows.shape[0], width), F32)], axis=0))
    lane = lax.broadcasted_iota(jnp.int32, (width, width), 1)
    row = lax.broadcasted_iota(jnp.int32, (width, width), 0)
    full = gram_ref[...]
    for k in range(2):
        place = width - 2 + k
        full = jnp.where(lane == place, jnp.broadcast_to(across[:, k : k + 1], full.shape), full)
        full = jnp.where(row == place, jnp.broadcast_to(rows[k : k + 1], full.shape), full)
    full_ref[...] = full

    def times_gram(t):
        return lax.dot_general(t, full_ref[...], NN, precision=HI)

    def half(i, t):
        t = orthonormal_rows(t)
        again = jnp.logical_and(i % 2 == 1, i < 2 * iters - 1)
        return lax.cond(again, times_gram, lambda t: t, t)

    t = lax.fori_loop(0, 2 * iters, half, times_gram(basis_ref[...]))
    last = jnp.broadcast_to(t[:, width - 1 : width], t.shape)
    out_ref[...] = jnp.broadcast_to(jnp.sum(t * last, axis=0, keepdims=True), out_ref.shape)


def pod_weights(gram, rows, basis):
    return pl.pallas_call(
        functools.partial(pod_kernel, POD_ITERS),
        out_shape=jax.ShapeDtypeStruct((8, gram.shape[0]), F32),
        in_specs=[VM] * 3,
        out_specs=VM,
        scratch_shapes=[pltpu.VMEM(gram.shape, F32)],
        name="pod",
    )(gram, rows, basis)


SIDES = [(ds, dv) for dv in (-1, 0, 1) for ds in (-1, 0, 1) if (ds, dv) != (0, 0)]
LONG = 8


def present(ds, dv):
    s, v = lax.axis_index("stream") + ds, lax.axis_index("vert") + dv
    inside_s = jnp.logical_and(s >= 0, s < lax.axis_size("stream"))
    return jnp.logical_and(inside_s, jnp.logical_and(v >= 0, v < lax.axis_size("vert")))


def halo_copy(own_ref, ext_ref, send_sem, recv_sem, index):
    blocks = own_ref.shape[0]
    ds, dv = SIDES[index]
    if ds == 0:
        source, target = own_ref, ext_ref.at[1 - dv, pl.ds(1, blocks)]
    elif ds == 1:
        source, target = own_ref.at[pl.ds(blocks - 1, 1)], ext_ref.at[1 - dv, pl.ds(0, 1)]
    else:
        source, target = own_ref.at[pl.ds(0, 1)], ext_ref.at[1 - dv, pl.ds(blocks + 1, 1)]
    return pltpu.make_async_remote_copy(
        src_ref=source,
        dst_ref=target,
        send_sem=send_sem.at[index],
        recv_sem=recv_sem.at[index],
        device_id=(lax.axis_index("stream") + ds, lax.axis_index("vert") + dv),
        device_id_type=MESH,
    )


def halo_greet(barrier):
    count = 0
    for ds, dv in SIDES:
        here = present(ds, dv)
        count = count + here.astype(jnp.int32)

        @pl.when(here)
        def _():
            device = (lax.axis_index("stream") + ds, lax.axis_index("vert") + dv)
            pl.semaphore_signal(barrier, inc=1, device_id=device, device_id_type=MESH)

    return count


def halo_start(own_ref, ext_ref, send_sem, recv_sem):
    blocks = own_ref.shape[0]
    for index in (1, 6, 0, 2, 3, 4, 5, 7):
        ds, dv = SIDES[index]

        @pl.when(present(ds, dv))
        def _():
            halo_copy(own_ref, ext_ref, send_sem, recv_sem, index).start()

        @pl.when(jnp.logical_not(present(ds, dv)))
        def _():
            if ds == 0:
                ext_ref[1 + dv, 1 : blocks + 1] = jnp.zeros(own_ref.shape, F32)
            else:
                ext_ref[1 + dv, 0 if ds < 0 else blocks + 1] = jnp.zeros(own_ref.shape[1:], F32)


def halo_finish(own_ref, ext_ref, send_sem, recv_sem):
    for index, (ds, dv) in enumerate(SIDES):
        back = SIDES.index((-ds, -dv))

        @pl.when(present(ds, dv))
        def _():
            halo_copy(own_ref, ext_ref, send_sem, recv_sem, index).wait_send()
            halo_copy(own_ref, ext_ref, send_sem, recv_sem, back).wait_recv()


def groups():
    stream, vert = lax.axis_index("stream"), lax.axis_index("vert")
    core, z, y = stream % 2, (stream // 2) % LONG, stream // (2 * LONG)
    return (
        (vert * 2 + core, lambda r: (stream - core + r % 2, r // 2)),
        (z, lambda r: (stream + (r - z) * 2, vert)),
        (y, lambda r: (stream + (r - y) * 2 * LONG, vert)),
    )


def group_greet(barrier, me, device):
    for step in range(1, LONG):
        pl.semaphore_signal(barrier, inc=1, device_id=device((me + step) % LONG), device_id_type=MESH)
    return LONG - 1


def group_copies(me, device, source, target, send_sem, recv_sem):
    copies = []
    for step in range(1, LONG):
        other = (me + step) % LONG
        copies.append(
            pltpu.make_async_remote_copy(
                src_ref=source(other),
                dst_ref=target(step),
                send_sem=send_sem.at[step],
                recv_sem=recv_sem.at[step],
                device_id=device(other),
                device_id_type=MESH,
            )
        )
    return copies


def start(copies):
    for copy in copies:
        copy.start()


def finish(copies):
    for copy in copies:
        copy.wait()


def total(own, slots_ref):
    for step in range(1, LONG):
        own = own + slots_ref[step]
    return own


def shard_of(index, size):
    return pl.ds(pl.multiple_of(index * size, size), size)


def first_kernel(own_ref, gram_ref, start_ref, ext_ref, part_ref, basis_ref, slots, local_sem, send, recv, gsend, grecv):
    near = groups()[0]
    size = gram_ref.shape[0] // LONG
    local = pltpu.make_async_copy(own_ref, ext_ref.at[1, pl.ds(1, own_ref.shape[0])], local_sem)
    local.start()
    barrier = pltpu.get_barrier_semaphore()
    pl.semaphore_wait(barrier, halo_greet(barrier) + group_greet(barrier, *near))
    halo_start(own_ref, ext_ref, send, recv)
    copies = group_copies(*near, lambda other: gram_ref.at[shard_of(other, size)], lambda step: slots.at[step], gsend, grecv)
    start(copies)
    basis_ref[...] = start_ref[...]

    @pl.loop(0, 2)
    def _(i):
        basis_ref[...] = orthonormal_rows(basis_ref[...])

    finish(copies)
    part_ref[...] = total(gram_ref[shard_of(near[0], size)], slots)
    halo_finish(own_ref, ext_ref, send, recv)
    local.wait()


def second_kernel(own_ref, part_ref, ext_ref, out_ref, slots, sums, local_sem, send, recv, gsend, grecv):
    _, z, y = groups()
    local = pltpu.make_async_copy(own_ref, ext_ref.at[1, pl.ds(1, own_ref.shape[0])], local_sem)
    local.start()
    barrier = pltpu.get_barrier_semaphore()
    pl.semaphore_wait(barrier, halo_greet(barrier) + group_greet(barrier, *z) + group_greet(barrier, *y))
    copies = group_copies(*z, lambda other: part_ref, lambda step: slots.at[0, step], gsend.at[0], grecv.at[0])
    start(copies)
    halo_start(own_ref, ext_ref, send, recv)
    finish(copies)
    sums[...] = total(part_ref[...], slots.at[0])
    copies = group_copies(*y, lambda other: sums, lambda step: slots.at[1, step], gsend.at[1], grecv.at[1])
    start(copies)
    halo_finish(own_ref, ext_ref, send, recv)
    finish(copies)
    out_ref[...] = total(sums[...], slots.at[1])
    local.wait()


def third_kernel(rows_ref, part_ref, rows_out, gram_out, slots, sums, send, recv, gsend, grecv, local_sem):
    near, z, y = groups()
    size = part_ref.shape[0]
    barrier = pltpu.get_barrier_semaphore()
    local = pltpu.make_async_copy(part_ref, gram_out.at[shard_of(near[0], size)], local_sem)
    local.start()
    pl.semaphore_wait(barrier, group_greet(barrier, *near) + group_greet(barrier, *z) + group_greet(barrier, *y))
    gathers = group_copies(*near, lambda other: part_ref, lambda step: gram_out.at[shard_of(near[0], size)], gsend, grecv)
    source, value = rows_ref, rows_ref[...]
    for stage, group in enumerate((z, y, near)):
        copies = group_copies(
            *group, lambda other: source, lambda step: slots.at[stage, step], send.at[stage], recv.at[stage]
        )
        start(copies)
        if stage == 0:
            start(gathers)
        finish(copies)
        value = total(value, slots.at[stage])
        if stage < 2:
            sums[stage] = value
            source = sums.at[stage]
    rows_out[...] = value
    finish(gathers)
    local.wait()


def remote(kernel, name, collective_id, operands, shapes, scratch):
    return pl.pallas_call(
        kernel,
        out_shape=[jax.ShapeDtypeStruct(shape, F32) for shape in shapes],
        in_specs=[VM] * len(operands),
        out_specs=[VM] * len(shapes),
        scratch_shapes=scratch,
        compiler_params=pltpu.CompilerParams(collective_id=collective_id, has_side_effects=True),
        name=name,
    )(*operands)


def body(particles, phase_flags, neighbours, history, basis_start):
    blocks, _, fields, part = particles.shape
    snaps, rank = basis_start.shape
    state = particles.reshape(blocks * fields, part)
    codes = neighbours[:, 0].T
    past = jnp.transpose(history[:, 0], (1, 2, 0, 3))
    dma = pltpu.SemaphoreType.DMA
    payload = prepare(state, phase_flags[:, 0])
    gram = jnp.einsum("csbp,ctbp->st", past, past, preferred_element_type=F32)
    gram = jnp.pad(gram, ((0, 2), (0, 2)))
    wide = (3, blocks + 2, 8, part)
    shard = snaps // LONG
    ext, piece, basis = remote(
        first_kernel, "first", 0, (payload, gram, basis_start.T), (wide, (shard, snaps), (rank, snaps)),
        [pltpu.VMEM((LONG, shard, snaps), F32), dma, dma((8,)), dma((8,)), dma((LONG,)), dma((LONG,))],
    )
    state, speed_1, payload = forces_step(codes, ext, state, False)
    ext, piece = remote(
        second_kernel, "second", 1, (payload, piece), (wide, (shard, snaps)),
        [pltpu.VMEM((2, LONG, shard, snaps), F32), pltpu.VMEM((shard, snaps), F32), dma, dma((8,)), dma((8,)),
         dma((2, LONG)), dma((2, LONG))],
    )
    state, speed_2 = forces_step(codes, ext, state, True)
    newest = jnp.stack([speed_1, speed_2]).astype(BF)
    with_past = jnp.einsum("kcbp,csbp->ks", newest, past, preferred_element_type=F32)
    with_newest = jnp.einsum("kcbp,lcbp->kl", newest, newest, preferred_element_type=F32)
    rows = jnp.pad(jnp.concatenate([with_past, with_newest], axis=1), ((0, 6), (0, 0)))
    rows, gram = remote(
        third_kernel, "third", 2, (rows, piece), ((8, snaps), (snaps, snaps)),
        [pltpu.VMEM((3, LONG, 8, snaps), F32), pltpu.VMEM((2, 8, snaps), F32), dma((3, LONG)), dma((3, LONG)),
         dma((LONG,)), dma((LONG,)), dma],
    )
    weights = pod_weights(gram, rows, basis)[0]
    filtered = jnp.sum(past.astype(F32) * weights[:-2, None, None], axis=1)
    for k in range(2):
        filtered = filtered + weights[snaps - 2 + k] * newest[k].astype(F32)
    filtered = jnp.transpose(filtered, (1, 0, 2))
    return (state.reshape(particles.shape), filtered[:, None])


def solution(mesh):
    in_specs = (
        P("stream", "vert", None, None),
        P("stream", "vert", None),
        P("stream", "vert", None),
        P("stream", "vert", None, None, None),
        P(),
    )
    out_specs = (P("stream", "vert", None, None), P("stream", "vert", None, None))
    return jax.shard_map(body, mesh=mesh, in_specs=in_specs, out_specs=out_specs, check_vma=False)
```

```python
import functools
import math

import jax
import jax.numpy as jnp
from jax import lax
from jax.experimental import pallas as pl
from jax.experimental.pallas import tpu as pltpu
from jax.sharding import PartitionSpec as P

POD_ITERS = 4
VOLUME = 1.0 / 16.0
STIFFNESS = 100.0 / 7.0
SLOPE = -5.0 * 21.0 / (16.0 * math.pi)
DT = 0.02
SEDIMENT_EXTRA = 1.65

HI = lax.Precision.HIGHEST
NT = (((1,), (1,)), ((), ()))
NN = (((1,), (0,)), ((), ()))
TN = (((0,), (0,)), ((), ()))
BF = jnp.bfloat16
F32 = jnp.float32
MESH = pl.DeviceIdType.MESH
VM = pl.BlockSpec(memory_space=pltpu.VMEM)

TRIP = 8


def pressure_of(relative, density):
    power = relative * relative
    power = power * power * power * relative
    return STIFFNESS * (power - 1.0) / (density * relative * relative)


def split3(x):
    a = x.astype(BF).astype(F32)
    b = (x - a).astype(BF).astype(F32)
    return a, b, x - a - b


def forces(codes_ref, ext_ref, state_ref, out_ref, speed_ref, next_ref=None):
    blocks, part = ext_ref.shape[1] - 2, ext_ref.shape[3]
    row = lax.broadcasted_iota(jnp.int32, (8, part), 0)

    def centred(vert, stream, ds, dv):
        field = ext_ref[vert, stream]
        shift = jnp.where(row == 0, 2.0 * ds - 1.0, jnp.where(row == 1, -1.0, jnp.where(row == 2, 2.0 * dv - 1.0, 0.0)))
        return field + shift

    def norm(half):
        square = half * half
        return square[0:1] + square[1:2] + square[2:3]

    def one_block(b):
        own = centred(1, b + 1, 0.0, 0.0)
        half = 0.5 * own
        target = jnp.where(row < 3, half, jnp.where(row == 3, 1.0, jnp.where(row == 4, norm(half), 0.0)))
        h, m, l = split3(target)
        target = jnp.concatenate([h, h, m, h, l, m], axis=0).astype(BF)
        lefts, rights = [], []
        for n in range(5):
            if n == 0:
                vert, stream, ds, dv = 1, b + 1, 0.0, 0.0
            else:
                code = codes_ref[n - 1, b]
                code = jnp.where(code >= 4, code + 1, code)
                third = lax.div(code, 3)
                ds, dv = third - 1, code - 3 * third - 1
                vert, stream = dv + 1, b + 1 + ds
                ds, dv = ds.astype(F32), dv.astype(F32)
            near = centred(vert, stream, ds, dv)
            half = 0.5 * near
            source = jnp.where(row < 3, -2.0 * half, jnp.where(row == 3, norm(half), jnp.where(row == 4, 1.0, 0.0)))
            h, m, l = split3(source)
            source = jnp.concatenate([h, m, h, l, h, m], axis=0).astype(BF)
            mass = near[6:7]
            weighted = jnp.where(row == 6, 1.0, near) * mass
            dots = near[0:3] * near[3:6]
            dot = mass * (dots[0:1] + dots[1:2] + dots[2:3])
            second = jnp.where(row < 3, weighted * near[7:8], jnp.where(row == 3, dot, 0.0))
            fields = jnp.concatenate([weighted, second], axis=0)
            high = fields.astype(BF)
            low = (fields - high.astype(F32)).astype(BF)
            quarter = lax.dot_general(target, source, TN, preferred_element_type=F32)
            quarter = jnp.maximum(quarter, 1e-30)
            reach = jnp.maximum(1.0 - quarter * lax.rsqrt(quarter), 0.0)
            cube = reach * reach * reach
            cube_high = cube.astype(BF)
            cube_low = (cube - cube_high.astype(F32)).astype(BF)
            left = jnp.concatenate([cube_high, cube_low], axis=1)
            right = jnp.concatenate([jnp.concatenate([high, high], axis=1), jnp.concatenate([low, jnp.zeros_like(low)], axis=1)], axis=0)
            lefts.append(left)
            rights.append(right)
        sums = lax.dot_general(jnp.concatenate(lefts, axis=1), jnp.concatenate(rights, axis=1), NT, preferred_element_type=F32)
        sums = jnp.transpose(sums)
        sums = sums[0:16] + sums[16:32]
        relative = state_ref[pl.ds(7 * b + 6, 1)]
        density = 16.0 * own[6:7]
        place, speed, pressure = own[0:3], own[3:6], own[7:8]
        total, pressure_total, vx = sums[6:7], sums[7:8], sums[11:12]
        dots = speed * (place * total - sums[0:3]) - place * sums[3:6]
        rate = SLOPE * (dots[0:1] + dots[1:2] + dots[2:3] + vx)
        acc = -SLOPE * (pressure * (place * total - sums[0:3]) + place * pressure_total - sums[8:11])
        gravity = jnp.where(row[0:3] == 2, -1.0, 0.0)
        speed = speed + DT * (acc + gravity)
        place = ext_ref[1, b + 1][0:3] + DT * speed
        relative = relative + DT * rate / density
        out_ref[pl.ds(7 * b, 7)] = jnp.concatenate([place, speed, relative], axis=0)
        for c in range(3):
            speed_ref[c, pl.ds(b, 1)] = speed[c : c + 1]
        if next_ref is not None:
            pressure = pressure_of(relative, density)
            next_ref[1, b + 1] = jnp.concatenate([place, speed, own[6:7], pressure], axis=0)

    def several(i, carry):
        for k in range(TRIP):
            one_block(TRIP * i + k)
        return carry

    lax.fori_loop(0, blocks // TRIP, several, 0)


def orthonormal_rows(t):
    rank, width = t.shape
    zero = jnp.zeros((width - rank, width), jnp.float32)
    lane = lax.broadcasted_iota(jnp.int32, (rank, width), 1)
    row = lax.broadcasted_iota(jnp.int32, (rank, width), 0)
    unit = jnp.where(lane == row + rank, 1.0, 0.0)
    work = lax.dot_general(t, jnp.concatenate([t, zero], axis=0), NT, precision=HI) + unit
    eight = lax.broadcasted_iota(jnp.int32, (8, width), 0)
    count = rank // 8

    groups = [work[8 * g:8 * g + 8] for g in range(count)]
    for p in range(count):
        live = range(p, count)
        cols = [{g: jnp.broadcast_to(groups[g][:, 8 * p + c:8 * p + c + 1], (8, width)) for g in live} for c in range(8)]
        for k in range(8):
            inv = lax.rsqrt(jnp.broadcast_to(cols[k][p][k:k + 1], (8, width)))
            low = {g: cols[k][g] * inv for g in live}
            pivot_row = jnp.broadcast_to(groups[p][k:k + 1], (8, width)) * inv
            for c in range(k + 1, 8):
                factor = jnp.broadcast_to(low[p][c:c + 1], (8, width))
                for g in live:
                    cols[c][g] = cols[c][g] - low[g] * factor
            groups[p] = jnp.where(eight == k, pivot_row, jnp.where(eight > k, groups[p] - low[p] * pivot_row, groups[p]))
            for g in range(p + 1, count):
                groups[g] = groups[g] - low[g] * pivot_row
    done = jnp.concatenate(groups, axis=0)
    return lax.dot_general(done, jnp.concatenate([zero, t], axis=0), NN, precision=HI)
SIDES = [(ds, dv) for dv in (-1, 0, 1) for ds in (-1, 0, 1) if (ds, dv) != (0, 0)]
LONG = 8


def present(ds, dv):
    s, v = lax.axis_index("stream") + ds, lax.axis_index("vert") + dv
    inside_s = jnp.logical_and(s >= 0, s < lax.axis_size("stream"))
    return jnp.logical_and(inside_s, jnp.logical_and(v >= 0, v < lax.axis_size("vert")))


def halo_copy(ext_ref, send_sem, recv_sem, index):
    blocks = ext_ref.shape[1] - 2
    ds, dv = SIDES[index]
    if ds == 0:
        source, target = pl.ds(1, blocks), pl.ds(1, blocks)
    elif ds == 1:
        source, target = pl.ds(blocks, 1), pl.ds(0, 1)
    else:
        source, target = pl.ds(1, 1), pl.ds(blocks + 1, 1)
    source, target = ext_ref.at[1, source], ext_ref.at[1 - dv, target]
    return pltpu.make_async_remote_copy(
        src_ref=source,
        dst_ref=target,
        send_sem=send_sem.at[index],
        recv_sem=recv_sem.at[index],
        device_id=(lax.axis_index("stream") + ds, lax.axis_index("vert") + dv),
        device_id_type=MESH,
    )


def halo_greet(barrier):
    count = 0
    for ds, dv in SIDES:
        here = present(ds, dv)
        count = count + here.astype(jnp.int32)

        @pl.when(here)
        def _():
            device = (lax.axis_index("stream") + ds, lax.axis_index("vert") + dv)
            pl.semaphore_signal(barrier, inc=1, device_id=device, device_id_type=MESH)

    return count


def halo_clear(ext_ref):
    blocks, fields, part = ext_ref.shape[1] - 2, ext_ref.shape[2], ext_ref.shape[3]
    for ds, dv in SIDES:

        @pl.when(jnp.logical_not(present(ds, dv)))
        def _():
            if ds == 0:
                ext_ref[1 + dv, 1 : blocks + 1] = jnp.zeros((blocks, fields, part), F32)
            else:
                ext_ref[1 + dv, 0 if ds < 0 else blocks + 1] = jnp.zeros((fields, part), F32)


def halo_start(ext_ref, send_sem, recv_sem):
    for index in (1, 6, 0, 2, 3, 4, 5, 7):

        @pl.when(present(*SIDES[index]))
        def _():
            halo_copy(ext_ref, send_sem, recv_sem, index).start()


def halo_finish(ext_ref, send_sem, recv_sem):
    for index, (ds, dv) in enumerate(SIDES):
        back = SIDES.index((-ds, -dv))

        @pl.when(present(ds, dv))
        def _():
            halo_copy(ext_ref, send_sem, recv_sem, index).wait_send()
            halo_copy(ext_ref, send_sem, recv_sem, back).wait_recv()


def groups():
    stream, vert = lax.axis_index("stream"), lax.axis_index("vert")
    core, z, y = stream % 2, (stream // 2) % LONG, stream // (2 * LONG)
    return (
        (vert * 2 + core, lambda r: (stream - core + r % 2, r // 2)),
        (z, lambda r: (stream + (r - z) * 2, vert)),
        (y, lambda r: (stream + (r - y) * 2 * LONG, vert)),
    )


def group_greet(barrier, me, device):
    for step in range(1, LONG):
        pl.semaphore_signal(barrier, inc=1, device_id=device((me + step) % LONG), device_id_type=MESH)
    return LONG - 1


def group_copies(me, device, source, target, send_sem, recv_sem):
    copies = []
    for step in range(1, LONG):
        other = (me + step) % LONG
        copies.append(
            pltpu.make_async_remote_copy(
                src_ref=source(other),
                dst_ref=target(step),
                send_sem=send_sem.at[step],
                recv_sem=recv_sem.at[step],
                device_id=device(other),
                device_id_type=MESH,
            )
        )
    return copies


def start(copies):
    for copy in copies:
        copy.start()


def finish(copies):
    for copy in copies:
        copy.wait()


def total(own, slots_ref):
    for step in range(1, LONG):
        own = own + slots_ref[step]
    return own


def shard_of(index, size):
    return pl.ds(pl.multiple_of(index * size, size), size)


def rounded(speed_ref):
    return [speed_ref[c].astype(BF).astype(F32) for c in range(3)]


def plane_products(planes, others, products_ref, s):
    acc = None
    for plane, other in zip(planes, others):
        term = plane * other
        acc = term if acc is None else acc + term
    blocks = acc.shape[0]
    folded = acc[0:8]
    for g in range(1, blocks // 8):
        folded = folded + acc[8 * g : 8 * g + 8]
    products_ref[pl.ds(pl.multiple_of(8 * s, 8), 8)] = folded


def inner_products(newest, past_ref, products_ref):
    past = past_ref.shape[1]

    def several(i, carry):
        for k in range(3):
            s = 3 * i + k
            plane_products(newest, [past_ref[c, s].astype(F32) for c in range(3)], products_ref, s)
        return carry

    lax.fori_loop(0, past // 3, several, 0)


def product_row(products_ref):
    snaps = products_ref.shape[0] // 8
    sums = products_ref[pl.ds(0, snaps, stride=8)]
    for q in range(1, 8):
        sums = sums + products_ref[pl.ds(q, snaps, stride=8)]
    return lax.dot_general(jnp.ones((8, sums.shape[1]), F32), sums, NT, precision=HI)


def flow_kernel(
    codes_ref, state_ref, flags_ref, gram_ref, start_ref, past_hbm,
    out_ref, speed_1, speed_2, rows_out, gram_out, basis_ref,
    ext_1, ext_2, middle, past, products, rows, piece, near_slots, long_slots, row_slots,
    past_sem, send_1, recv_1, send_2, recv_2, near_send, near_recv, long_send, long_recv,
    all_send, all_recv, row_send, row_recv,
):
    near, z, y = groups()
    blocks, part = flags_ref.shape
    snaps = gram_ref.shape[0]
    size = snaps // LONG
    load = pltpu.make_async_copy(past_hbm, past, past_sem)
    load.start()
    barrier = pltpu.get_barrier_semaphore()
    count = halo_greet(barrier)
    for group in (near, z, y):
        count = count + group_greet(barrier, *group)
    density = 1.0 + SEDIMENT_EXTRA * flags_ref[...].astype(F32)
    mass = density * VOLUME
    pressure = pressure_of(state_ref[pl.ds(6, blocks, stride=7)], density)
    for b in range(blocks):
        ext_1[1, b + 1, 0:6] = state_ref[7 * b : 7 * b + 6]
        ext_1[1, b + 1, 6:7] = mass[b : b + 1]
        ext_1[1, b + 1, 7:8] = pressure[b : b + 1]
    halo_clear(ext_1)
    halo_clear(ext_2)
    products[pl.ds(8 * (snaps - 2), 16)] = jnp.zeros((16, part), F32)
    pl.semaphore_wait(barrier, count)

    halo_start(ext_1, send_1, recv_1)
    scatter = group_copies(
        *near, lambda other: gram_ref.at[shard_of(other, size)], lambda step: near_slots.at[step], near_send, near_recv
    )
    start(scatter)
    basis_ref[...] = start_ref[...]

    @pl.loop(0, 2)
    def _(i):
        basis_ref[...] = orthonormal_rows(basis_ref[...])

    halo_finish(ext_1, send_1, recv_1)
    forces(codes_ref, ext_1, state_ref, middle, speed_1, ext_2)

    finish(scatter)
    piece[0] = total(gram_ref[shard_of(near[0], size)], near_slots)
    over_z = group_copies(*z, lambda other: piece.at[0], lambda step: long_slots.at[0, step], long_send.at[0], long_recv.at[0])
    halo_start(ext_2, send_2, recv_2)
    start(over_z)
    load.wait()
    first = rounded(speed_1)
    inner_products(first, past, products)
    plane_products(first, first, products, snaps - 2)
    rows[0] = product_row(products)
    finish(over_z)
    piece[1] = total(piece[0], long_slots.at[0])
    over_y = group_copies(*y, lambda other: piece.at[1], lambda step: long_slots.at[1, step], long_send.at[1], long_recv.at[1])
    start(over_y)
    halo_finish(ext_2, send_2, recv_2)
    forces(codes_ref, ext_2, middle, out_ref, speed_2)

    finish(over_y)
    whole = total(piece[1], long_slots.at[1])
    piece[2] = whole
    gram_out[shard_of(near[0], size)] = whole
    second = rounded(speed_2)
    inner_products(second, past, products)
    plane_products(second, rounded(speed_1), products, snaps - 2)
    plane_products(second, second, products, snaps - 1)
    eight = lax.broadcasted_iota(jnp.int32, (8, snaps), 0)
    value = jnp.where(eight == 0, rows[0], product_row(products))
    gathers = group_copies(*near, lambda other: piece.at[2], lambda step: gram_out.at[shard_of(near[0], size)], all_send, all_recv)
    for stage, group in enumerate((z, y, near)):
        rows[1 + stage] = value
        copies = group_copies(
            *group, lambda other: rows.at[1 + stage], lambda step: row_slots.at[stage, step],
            row_send.at[stage], row_recv.at[stage],
        )
        start(copies)
        if stage == 0:
            start(gathers)
        finish(copies)
        value = total(value, row_slots.at[stage])
    rows_out[...] = value
    finish(gathers)


def flow(codes, state, flags, gram, start_rows, past):
    blocks, part = flags.shape
    rank, snaps = start_rows.shape
    shard = snaps // LONG
    dma = pltpu.SemaphoreType.DMA
    ext = pltpu.VMEM((3, blocks + 2, 8, part), F32)
    shapes = [state.shape, (3, blocks, part), (3, blocks, part), (8, snaps), (snaps, snaps), (rank, snaps)]
    return pl.pallas_call(
        flow_kernel,
        out_shape=[jax.ShapeDtypeStruct(shape, F32) for shape in shapes],
        in_specs=[pl.BlockSpec(memory_space=pltpu.SMEM), VM, VM, VM, VM, pl.BlockSpec(memory_space=pl.ANY)],
        out_specs=[VM] * len(shapes),
        scratch_shapes=[
            ext, ext,
            pltpu.VMEM(state.shape, F32),
            pltpu.VMEM(past.shape, BF),
            pltpu.VMEM((8 * snaps, part), F32),
            pltpu.VMEM((4, 8, snaps), F32),
            pltpu.VMEM((3, shard, snaps), F32),
            pltpu.VMEM((LONG, shard, snaps), F32),
            pltpu.VMEM((2, LONG, shard, snaps), F32),
            pltpu.VMEM((3, LONG, 8, snaps), F32),
            dma, dma((8,)), dma((8,)), dma((8,)), dma((8,)), dma((LONG,)), dma((LONG,)), dma((2, LONG)), dma((2, LONG)),
            dma((LONG,)), dma((LONG,)), dma((3, LONG)), dma((3, LONG)),
        ],
        compiler_params=pltpu.CompilerParams(collective_id=0, has_side_effects=True),
        name="flow",
    )(codes, state, flags, gram, start_rows, past)


def modes_kernel(gram_ref, rows_ref, basis_ref, speed_1, speed_2, past_hbm, out_ref, full_ref, past, weights, past_sem):
    width = gram_ref.shape[0]
    load = pltpu.make_async_copy(past_hbm, past, past_sem)
    load.start()
    rows = rows_ref[...]
    across = jnp.transpose(jnp.concatenate([rows, jnp.zeros((width - rows.shape[0], width), F32)], axis=0))
    lane = lax.broadcasted_iota(jnp.int32, (width, width), 1)
    row = lax.broadcasted_iota(jnp.int32, (width, width), 0)
    full = gram_ref[...]
    for k in range(2):
        place = width - 2 + k
        full = jnp.where(lane == place, jnp.broadcast_to(across[:, k : k + 1], full.shape), full)
        full = jnp.where(row == place, jnp.broadcast_to(rows[k : k + 1], full.shape), full)
    full_ref[...] = full

    def times_gram(t):
        return lax.dot_general(t, full_ref[...], NN, precision=HI)

    def half(i, t):
        t = orthonormal_rows(t)
        again = jnp.logical_and(i % 2 == 1, i < 2 * POD_ITERS - 1)
        return lax.cond(again, times_gram, lambda t: t, t)

    t = lax.fori_loop(0, 2 * POD_ITERS, half, times_gram(basis_ref[...]))
    last = jnp.broadcast_to(t[:, width - 1 : width], t.shape)
    weights[...] = lax.dot_general(t, last, TN, precision=HI)
    load.wait()
    snaps = past.shape[1]

    def several(i, sums):
        for k in range(3):
            s = 3 * i + k
            weight = jnp.broadcast_to(weights[pl.ds(s, 1)], sums[0].shape)
            sums = tuple(total + past[c, s].astype(F32) * weight for c, total in enumerate(sums))
        return sums

    zero = jnp.zeros(speed_1.shape[1:], F32)
    sums = lax.fori_loop(0, snaps // 3, several, (zero, zero, zero))
    for k, speed_ref in enumerate((speed_1, speed_2)):
        weight = jnp.broadcast_to(weights[width - 2 + k : width - 1 + k], zero.shape)
        sums = [total + plane * weight for total, plane in zip(sums, rounded(speed_ref))]
    for c in range(3):
        out_ref[pl.ds(c, zero.shape[0], stride=3)] = sums[c]


def modes(gram, rows, basis, speed_1, speed_2, past):
    components, _, blocks, part = past.shape
    return pl.pallas_call(
        modes_kernel,
        out_shape=jax.ShapeDtypeStruct((components * blocks, part), F32),
        in_specs=[VM] * 5 + [pl.BlockSpec(memory_space=pl.ANY)],
        out_specs=VM,
        scratch_shapes=[
            pltpu.VMEM(gram.shape, F32),
            pltpu.VMEM(past.shape, BF),
            pltpu.VMEM(gram.shape, F32),
            pltpu.SemaphoreType.DMA,
        ],
        name="modes",
    )(gram, rows, basis, speed_1, speed_2, past)


def body(particles, phase_flags, neighbours, history, basis_start):
    blocks, _, fields, part = particles.shape
    state = particles.reshape(blocks * fields, part)
    past = jnp.transpose(history[:, 0], (1, 2, 0, 3))
    gram = jnp.einsum("csbp,ctbp->st", past, past, preferred_element_type=F32)
    gram = jnp.pad(gram, ((0, 2), (0, 2)))
    state, speed_1, speed_2, rows, gram, basis = flow(
        neighbours[:, 0].T, state, phase_flags[:, 0], gram, basis_start.T, past
    )
    filtered = modes(gram, rows, basis, speed_1, speed_2, past)
    return (state.reshape(particles.shape), filtered.reshape(blocks, 1, 3, part))


def solution(mesh):
    in_specs = (
        P("stream", "vert", None, None),
        P("stream", "vert", None),
        P("stream", "vert", None),
        P("stream", "vert", None, None, None),
        P(),
    )
    out_specs = (P("stream", "vert", None, None), P("stream", "vert", None, None))
    return jax.shard_map(body, mesh=mesh, in_specs=in_specs, out_specs=out_specs, check_vma=False)
```

```python
import functools
import math

import jax
import jax.numpy as jnp
from jax import lax
from jax.experimental import pallas as pl
from jax.experimental.pallas import tpu as pltpu
from jax.sharding import PartitionSpec as P

POD_ITERS = 4
VOLUME = 1.0 / 16.0
STIFFNESS = 100.0 / 7.0
SLOPE = -5.0 * 21.0 / (16.0 * math.pi)
DT = 0.02
SEDIMENT_EXTRA = 1.65

HI = lax.Precision.HIGHEST
NT = (((1,), (1,)), ((), ()))
NN = (((1,), (0,)), ((), ()))
TN = (((0,), (0,)), ((), ()))
BF = jnp.bfloat16
F32 = jnp.float32
MESH = pl.DeviceIdType.MESH
VM = pl.BlockSpec(memory_space=pltpu.VMEM)

TRIP = 8


def pressure_of(relative, density):
    power = relative * relative
    power = power * power * power * relative
    return STIFFNESS * (power - 1.0) / (density * relative * relative)


def split3(x):
    a = x.astype(BF).astype(F32)
    b = (x - a).astype(BF).astype(F32)
    return a, b, x - a - b


def forces(codes_ref, ext_ref, state_ref, out_ref, speed_ref, next_ref=None):
    blocks, part = ext_ref.shape[1] - 2, ext_ref.shape[3]
    row = lax.broadcasted_iota(jnp.int32, (8, part), 0)

    def centred(vert, stream, ds, dv):
        field = ext_ref[vert, stream]
        shift = jnp.where(row == 0, 2.0 * ds - 1.0, jnp.where(row == 1, -1.0, jnp.where(row == 2, 2.0 * dv - 1.0, 0.0)))
        return field + shift

    def norm(half):
        square = half * half
        return square[0:1] + square[1:2] + square[2:3]

    def one_block(b):
        own = centred(1, b + 1, 0.0, 0.0)
        half = 0.5 * own
        target = jnp.where(row < 3, half, jnp.where(row == 3, 1.0, jnp.where(row == 4, norm(half), 0.0)))
        h, m, l = split3(target)
        target = jnp.concatenate([h, h, m, h, l, m], axis=0).astype(BF)
        lefts, rights = [], []
        for n in range(5):
            if n == 0:
                vert, stream, ds, dv = 1, b + 1, 0.0, 0.0
            else:
                code = codes_ref[n - 1, b]
                code = jnp.where(code >= 4, code + 1, code)
                third = lax.div(code, 3)
                ds, dv = third - 1, code - 3 * third - 1
                vert, stream = dv + 1, b + 1 + ds
                ds, dv = ds.astype(F32), dv.astype(F32)
            near = centred(vert, stream, ds, dv)
            half = 0.5 * near
            source = jnp.where(row < 3, -2.0 * half, jnp.where(row == 3, norm(half), jnp.where(row == 4, 1.0, 0.0)))
            h, m, l = split3(source)
            source = jnp.concatenate([h, m, h, l, h, m], axis=0).astype(BF)
            mass = near[6:7]
            weighted = jnp.where(row == 6, 1.0, near) * mass
            dots = near[0:3] * near[3:6]
            dot = mass * (dots[0:1] + dots[1:2] + dots[2:3])
            second = jnp.where(row < 3, weighted * near[7:8], jnp.where(row == 3, dot, 0.0))
            fields = jnp.concatenate([weighted, second], axis=0)
            high = fields.astype(BF)
            low = (fields - high.astype(F32)).astype(BF)
            quarter = lax.dot_general(target, source, TN, preferred_element_type=F32)
            quarter = jnp.maximum(quarter, 1e-30)
            reach = jnp.maximum(1.0 - quarter * lax.rsqrt(quarter), 0.0)
            cube = reach * reach * reach
            cube_high = cube.astype(BF)
            cube_low = (cube - cube_high.astype(F32)).astype(BF)
            left = jnp.concatenate([cube_high, cube_low], axis=1)
            right = jnp.concatenate([jnp.concatenate([high, high], axis=1), jnp.concatenate([low, jnp.zeros_like(low)], axis=1)], axis=0)
            lefts.append(left)
            rights.append(right)
        sums = lax.dot_general(jnp.concatenate(lefts, axis=1), jnp.concatenate(rights, axis=1), NT, preferred_element_type=F32)
        sums = jnp.transpose(sums)
        sums = sums[0:16] + sums[16:32]
        relative = state_ref[pl.ds(7 * b + 6, 1)]
        density = 16.0 * own[6:7]
        place, speed, pressure = own[0:3], own[3:6], own[7:8]
        total, pressure_total, vx = sums[6:7], sums[7:8], sums[11:12]
        dots = speed * (place * total - sums[0:3]) - place * sums[3:6]
        rate = SLOPE * (dots[0:1] + dots[1:2] + dots[2:3] + vx)
        acc = -SLOPE * (pressure * (place * total - sums[0:3]) + place * pressure_total - sums[8:11])
        gravity = jnp.where(row[0:3] == 2, -1.0, 0.0)
        speed = speed + DT * (acc + gravity)
        place = ext_ref[1, b + 1][0:3] + DT * speed
        relative = relative + DT * rate / density
        out_ref[pl.ds(7 * b, 7)] = jnp.concatenate([place, speed, relative], axis=0)
        for c in range(3):
            speed_ref[c, pl.ds(b, 1)] = speed[c : c + 1]
        if next_ref is not None:
            pressure = pressure_of(relative, density)
            next_ref[1, b + 1] = jnp.concatenate([place, speed, own[6:7], pressure], axis=0)

    def several(i, carry):
        for k in range(TRIP):
            one_block(TRIP * i + k)
        return carry

    lax.fori_loop(0, blocks // TRIP, several, 0)


def orthonormal_rows(t):
    rank, width = t.shape
    zero = jnp.zeros((width - rank, width), jnp.float32)
    lane = lax.broadcasted_iota(jnp.int32, (rank, width), 1)
    row = lax.broadcasted_iota(jnp.int32, (rank, width), 0)
    unit = jnp.where(lane == row + rank, 1.0, 0.0)
    work = lax.dot_general(t, jnp.concatenate([t, zero], axis=0), NT, precision=HI) + unit
    eight = lax.broadcasted_iota(jnp.int32, (8, width), 0)
    count = rank // 8

    groups = [work[8 * g:8 * g + 8] for g in range(count)]
    for p in range(count):
        live = range(p, count)
        cols = [{g: jnp.broadcast_to(groups[g][:, 8 * p + c:8 * p + c + 1], (8, width)) for g in live} for c in range(8)]
        for k in range(8):
            inv = lax.rsqrt(jnp.broadcast_to(cols[k][p][k:k + 1], (8, width)))
            low = {g: cols[k][g] * inv for g in live}
            pivot_row = jnp.broadcast_to(groups[p][k:k + 1], (8, width)) * inv
            for c in range(k + 1, 8):
                factor = jnp.broadcast_to(low[p][c:c + 1], (8, width))
                for g in live:
                    cols[c][g] = cols[c][g] - low[g] * factor
            groups[p] = jnp.where(eight == k, pivot_row, jnp.where(eight > k, groups[p] - low[p] * pivot_row, groups[p]))
            for g in range(p + 1, count):
                groups[g] = groups[g] - low[g] * pivot_row
    done = jnp.concatenate(groups, axis=0)
    return lax.dot_general(done, jnp.concatenate([zero, t], axis=0), NN, precision=HI)
SIDES = [(ds, dv) for dv in (-1, 0, 1) for ds in (-1, 0, 1) if (ds, dv) != (0, 0)]
LONG = 8
JOIN = 8


def present(ds, dv):
    s, v = lax.axis_index("stream") + ds, lax.axis_index("vert") + dv
    inside_s = jnp.logical_and(s >= 0, s < lax.axis_size("stream"))
    return jnp.logical_and(inside_s, jnp.logical_and(v >= 0, v < lax.axis_size("vert")))


def halo_copy(ext_ref, send_sem, recv_sem, index):
    blocks = ext_ref.shape[1] - 2
    ds, dv = SIDES[index]
    if ds == 0:
        source, target = pl.ds(1, blocks), pl.ds(1, blocks)
    elif ds == 1:
        source, target = pl.ds(blocks, 1), pl.ds(0, 1)
    else:
        source, target = pl.ds(1, 1), pl.ds(blocks + 1, 1)
    source, target = ext_ref.at[1, source], ext_ref.at[1 - dv, target]
    return pltpu.make_async_remote_copy(
        src_ref=source,
        dst_ref=target,
        send_sem=send_sem.at[index],
        recv_sem=recv_sem.at[index],
        device_id=(lax.axis_index("stream") + ds, lax.axis_index("vert") + dv),
        device_id_type=MESH,
    )


def halo_greet(barrier):
    count = 0
    for ds, dv in SIDES:
        here = present(ds, dv)
        count = count + here.astype(jnp.int32)

        @pl.when(here)
        def _():
            device = (lax.axis_index("stream") + ds, lax.axis_index("vert") + dv)
            pl.semaphore_signal(barrier, inc=1, device_id=device, device_id_type=MESH)

    return count


def halo_clear(ext_ref):
    blocks, fields, part = ext_ref.shape[1] - 2, ext_ref.shape[2], ext_ref.shape[3]
    for ds, dv in SIDES:

        @pl.when(jnp.logical_not(present(ds, dv)))
        def _():
            if ds == 0:
                ext_ref[1 + dv, 1 : blocks + 1] = jnp.zeros((blocks, fields, part), F32)
            else:
                ext_ref[1 + dv, 0 if ds < 0 else blocks + 1] = jnp.zeros((fields, part), F32)


def halo_start(ext_ref, send_sem, recv_sem):
    for index in (1, 6, 0, 2, 3, 4, 5, 7):

        @pl.when(present(*SIDES[index]))
        def _():
            halo_copy(ext_ref, send_sem, recv_sem, index).start()


def halo_finish(ext_ref, send_sem, recv_sem):
    for index, (ds, dv) in enumerate(SIDES):
        back = SIDES.index((-ds, -dv))

        @pl.when(present(ds, dv))
        def _():
            halo_copy(ext_ref, send_sem, recv_sem, index).wait_send()
            halo_copy(ext_ref, send_sem, recv_sem, back).wait_recv()


def groups():
    stream, vert = lax.axis_index("stream"), lax.axis_index("vert")
    core, z, y = stream % 2, (stream // 2) % LONG, stream // (2 * LONG)
    return (
        (vert * 2 + core, lambda r: (stream - core + r % 2, r // 2)),
        (z, lambda r: (stream + (r - z) * 2, vert)),
        (y, lambda r: (stream + (r - y) * 2 * LONG, vert)),
    )


def group_greet(barrier, me, device):
    for step in range(1, LONG):
        pl.semaphore_signal(barrier, inc=1, device_id=device((me + step) % LONG), device_id_type=MESH)
    return LONG - 1


def group_copies(me, device, source, target, send_sem, recv_sem):
    copies = []
    for step in range(1, LONG):
        other = (me + step) % LONG
        copies.append(
            pltpu.make_async_remote_copy(
                src_ref=source(other),
                dst_ref=target(step),
                send_sem=send_sem.at[step],
                recv_sem=recv_sem.at[step],
                device_id=device(other),
                device_id_type=MESH,
            )
        )
    return copies


def start(copies):
    for copy in copies:
        copy.start()


def finish(copies):
    for copy in copies:
        copy.wait()


def total(own, slots_ref):
    for step in range(1, LONG):
        own = own + slots_ref[step]
    return own


def shard_of(index, size):
    return pl.ds(pl.multiple_of(index * size, size), size)


def rounded(speed_ref):
    return [speed_ref[c].astype(BF).astype(F32) for c in range(3)]


def plane_products(planes, others, products_ref, s):
    acc = None
    for plane, other in zip(planes, others):
        term = plane * other
        acc = term if acc is None else acc + term
    blocks = acc.shape[0]
    folded = acc[0:8]
    for g in range(1, blocks // 8):
        folded = folded + acc[8 * g : 8 * g + 8]
    products_ref[pl.ds(pl.multiple_of(8 * s, 8), 8)] = folded


def inner_products(newest, past_ref, products_ref):
    past = past_ref.shape[1]

    def several(i, carry):
        for k in range(3):
            s = 3 * i + k
            plane_products(newest, [past_ref[c, s].astype(F32) for c in range(3)], products_ref, s)
        return carry

    lax.fori_loop(0, past // 3, several, 0)


def product_row(products_ref):
    snaps = products_ref.shape[0] // 8
    sums = products_ref[pl.ds(0, snaps, stride=8)]
    for q in range(1, 8):
        sums = sums + products_ref[pl.ds(q, snaps, stride=8)]
    return lax.dot_general(jnp.ones((8, sums.shape[1]), F32), sums, NT, precision=HI)


def past_gram(past_ref, gram_ref):
    past, blocks = past_ref.shape[1], past_ref.shape[2]
    gram_ref[...] = jnp.zeros(gram_ref.shape, F32)
    sums = jnp.zeros((past, past), F32)
    for c in range(past_ref.shape[0]):
        planes = jnp.swapaxes(past_ref[c], 0, 1)
        for b in range(0, blocks, JOIN):
            joined = jnp.concatenate([planes[b + k] for k in range(JOIN)], axis=1)
            sums = sums + lax.dot_general(joined, joined, NT, preferred_element_type=F32)
    gram_ref[0:past, 0:past] = sums


def modes(gram_ref, rows, basis_ref, speed_1, speed_2, past, out_ref, full_ref, weights):
    width = gram_ref.shape[0]
    across = jnp.transpose(jnp.concatenate([rows, jnp.zeros((width - rows.shape[0], width), F32)], axis=0))
    lane = lax.broadcasted_iota(jnp.int32, (width, width), 1)
    row = lax.broadcasted_iota(jnp.int32, (width, width), 0)
    full = gram_ref[...]
    for k in range(2):
        place = width - 2 + k
        full = jnp.where(lane == place, jnp.broadcast_to(across[:, k : k + 1], full.shape), full)
        full = jnp.where(row == place, jnp.broadcast_to(rows[k : k + 1], full.shape), full)
    full_ref[...] = full

    def times_gram(t):
        return lax.dot_general(t, full_ref[...], NN, precision=HI)

    def half(i, t):
        t = orthonormal_rows(t)
        again = jnp.logical_and(i % 2 == 1, i < 2 * POD_ITERS - 1)
        return lax.cond(again, times_gram, lambda t: t, t)

    t = lax.fori_loop(0, 2 * POD_ITERS, half, times_gram(basis_ref[...]))
    last = jnp.broadcast_to(t[:, width - 1 : width], t.shape)
    weights[...] = lax.dot_general(t, last, TN, precision=HI)
    snaps = past.shape[1]

    def several(i, sums):
        for k in range(3):
            s = 3 * i + k
            weight = jnp.broadcast_to(weights[pl.ds(s, 1)], sums[0].shape)
            sums = tuple(total + past[c, s].astype(F32) * weight for c, total in enumerate(sums))
        return sums

    zero = jnp.zeros(speed_1.shape[1:], F32)
    sums = lax.fori_loop(0, snaps // 3, several, (zero, zero, zero))
    for k, speed_ref in enumerate((speed_1, speed_2)):
        weight = jnp.broadcast_to(weights[width - 2 + k : width - 1 + k], zero.shape)
        sums = [total + plane * weight for total, plane in zip(sums, rounded(speed_ref))]
    for c in range(3):
        out_ref[pl.ds(c, zero.shape[0], stride=3)] = sums[c]


def flow_kernel(
    codes_ref, state_ref, flags_ref, start_ref, past_hbm,
    out_ref, filtered_ref, speed_1, speed_2, gram_out, basis_ref, full, weights,
    gram_ref, ext_1, ext_2, middle, past, products, rows, piece, near_slots, long_slots, row_slots,
    past_sem, send_1, recv_1, send_2, recv_2, near_send, near_recv, long_send, long_recv,
    all_send, all_recv, row_send, row_recv,
):
    near, z, y = groups()
    blocks, part = flags_ref.shape
    snaps = gram_ref.shape[0]
    size = snaps // LONG
    load = pltpu.make_async_copy(past_hbm, past, past_sem)
    load.start()
    barrier = pltpu.get_barrier_semaphore()
    count = halo_greet(barrier)
    for group in (near, z, y):
        count = count + group_greet(barrier, *group)
    density = 1.0 + SEDIMENT_EXTRA * flags_ref[...].astype(F32)
    mass = density * VOLUME
    pressure = pressure_of(state_ref[pl.ds(6, blocks, stride=7)], density)
    for b in range(blocks):
        ext_1[1, b + 1, 0:6] = state_ref[7 * b : 7 * b + 6]
        ext_1[1, b + 1, 6:7] = mass[b : b + 1]
        ext_1[1, b + 1, 7:8] = pressure[b : b + 1]
    halo_clear(ext_1)
    halo_clear(ext_2)
    products[pl.ds(8 * (snaps - 2), 16)] = jnp.zeros((16, part), F32)
    load.wait()
    past_gram(past, gram_ref)
    pl.semaphore_wait(barrier, count)

    halo_start(ext_1, send_1, recv_1)
    scatter = group_copies(
        *near, lambda other: gram_ref.at[shard_of(other, size)], lambda step: near_slots.at[step], near_send, near_recv
    )
    start(scatter)
    basis_ref[...] = start_ref[...]

    @pl.loop(0, 2)
    def _(i):
        basis_ref[...] = orthonormal_rows(basis_ref[...])

    halo_finish(ext_1, send_1, recv_1)
    forces(codes_ref, ext_1, state_ref, middle, speed_1, ext_2)

    finish(scatter)
    piece[0] = total(gram_ref[shard_of(near[0], size)], near_slots)
    over_z = group_copies(*z, lambda other: piece.at[0], lambda step: long_slots.at[0, step], long_send.at[0], long_recv.at[0])
    halo_start(ext_2, send_2, recv_2)
    start(over_z)
    first = rounded(speed_1)
    inner_products(first, past, products)
    plane_products(first, first, products, snaps - 2)
    rows[0] = product_row(products)
    finish(over_z)
    piece[1] = total(piece[0], long_slots.at[0])
    over_y = group_copies(*y, lambda other: piece.at[1], lambda step: long_slots.at[1, step], long_send.at[1], long_recv.at[1])
    start(over_y)
    halo_finish(ext_2, send_2, recv_2)
    forces(codes_ref, ext_2, middle, out_ref, speed_2)

    finish(over_y)
    whole = total(piece[1], long_slots.at[1])
    piece[2] = whole
    gram_out[shard_of(near[0], size)] = whole
    second = rounded(speed_2)
    inner_products(second, past, products)
    plane_products(second, rounded(speed_1), products, snaps - 2)
    plane_products(second, second, products, snaps - 1)
    eight = lax.broadcasted_iota(jnp.int32, (8, snaps), 0)
    value = jnp.where(eight == 0, rows[0], product_row(products))
    gathers = group_copies(*near, lambda other: piece.at[2], lambda step: gram_out.at[shard_of(near[0], size)], all_send, all_recv)
    for stage, group in enumerate((z, y, near)):
        rows[1 + stage] = value
        copies = group_copies(
            *group, lambda other: rows.at[1 + stage], lambda step: row_slots.at[stage, step],
            row_send.at[stage], row_recv.at[stage],
        )
        start(copies)
        if stage == 0:
            start(gathers)
        finish(copies)
        value = total(value, row_slots.at[stage])
    rows[4] = value
    finish(gathers)
    modes(gram_out, rows[4], basis_ref, speed_1, speed_2, past, filtered_ref, full, weights)


def flow(codes, state, flags, start_rows, past):
    blocks, part = flags.shape
    rank, snaps = start_rows.shape
    shard = snaps // LONG
    dma = pltpu.SemaphoreType.DMA
    ext = pltpu.VMEM((3, blocks + 2, 8, part), F32)
    shapes = [state.shape, (3 * blocks, part)]
    square, speed = pltpu.VMEM((snaps, snaps), F32), pltpu.VMEM((3, blocks, part), F32)
    return pl.pallas_call(
        flow_kernel,
        out_shape=[jax.ShapeDtypeStruct(shape, F32) for shape in shapes],
        in_specs=[pl.BlockSpec(memory_space=pltpu.SMEM), VM, VM, VM, pl.BlockSpec(memory_space=pl.ANY)],
        out_specs=[VM] * len(shapes),
        scratch_shapes=[
            speed, speed, square, pltpu.VMEM((rank, snaps), F32), square, square, square,
            ext, ext,
            pltpu.VMEM(state.shape, F32),
            pltpu.VMEM(past.shape, BF),
            pltpu.VMEM((8 * snaps, part), F32),
            pltpu.VMEM((5, 8, snaps), F32),
            pltpu.VMEM((3, shard, snaps), F32),
            pltpu.VMEM((LONG, shard, snaps), F32),
            pltpu.VMEM((2, LONG, shard, snaps), F32),
            pltpu.VMEM((3, LONG, 8, snaps), F32),
            dma, dma((8,)), dma((8,)), dma((8,)), dma((8,)), dma((LONG,)), dma((LONG,)), dma((2, LONG)), dma((2, LONG)),
            dma((LONG,)), dma((LONG,)), dma((3, LONG)), dma((3, LONG)),
        ],
        compiler_params=pltpu.CompilerParams(collective_id=0, has_side_effects=True),
        name="flow",
    )(codes, state, flags, start_rows, past)


def body(particles, phase_flags, neighbours, history, basis_start):
    blocks, _, fields, part = particles.shape
    state = particles.reshape(blocks * fields, part)
    past = jnp.transpose(history[:, 0], (1, 2, 0, 3))
    state, filtered = flow(
        neighbours[:, 0].T, state, phase_flags[:, 0], basis_start.T, past
    )
    return (state.reshape(particles.shape), filtered.reshape(blocks, 1, 3, part))


def solution(mesh):
    in_specs = (
        P("stream", "vert", None, None),
        P("stream", "vert", None),
        P("stream", "vert", None),
        P("stream", "vert", None, None, None),
        P(),
    )
    out_specs = (P("stream", "vert", None, None), P("stream", "vert", None, None))
    return jax.shard_map(body, mesh=mesh, in_specs=in_specs, out_specs=out_specs, check_vma=False)
```

```python
import functools
import math

import jax
import jax.numpy as jnp
from jax import lax
from jax.experimental import pallas as pl
from jax.experimental.pallas import tpu as pltpu
from jax.sharding import PartitionSpec as P

POD_ITERS = 4
VOLUME = 1.0 / 16.0
STIFFNESS = 100.0 / 7.0
SLOPE = -5.0 * 21.0 / (16.0 * math.pi)
DT = 0.02
SEDIMENT_EXTRA = 1.65

HI = lax.Precision.HIGHEST
NT = (((1,), (1,)), ((), ()))
NN = (((1,), (0,)), ((), ()))
TN = (((0,), (0,)), ((), ()))
BF = jnp.bfloat16
F32 = jnp.float32
MESH = pl.DeviceIdType.MESH
VM = pl.BlockSpec(memory_space=pltpu.VMEM)

TRIP = 8


def pressure_of(relative, density):
    power = relative * relative
    power = power * power * power * relative
    return STIFFNESS * (power - 1.0) / (density * relative * relative)


def split3(x):
    a = x.astype(BF).astype(F32)
    b = (x - a).astype(BF).astype(F32)
    return a, b, x - a - b


def forces(codes_ref, ext_ref, state_ref, out_ref, speed_ref, next_ref=None, after_trip=None):
    blocks, part = ext_ref.shape[1] - 2, ext_ref.shape[3]
    row = lax.broadcasted_iota(jnp.int32, (8, part), 0)

    def centred(vert, stream, ds, dv):
        field = ext_ref[vert, stream]
        shift = jnp.where(row == 0, 2.0 * ds - 1.0, jnp.where(row == 1, -1.0, jnp.where(row == 2, 2.0 * dv - 1.0, 0.0)))
        return field + shift

    def norm(half):
        square = half * half
        return square[0:1] + square[1:2] + square[2:3]

    def one_block(b):
        own = centred(1, b + 1, 0.0, 0.0)
        half = 0.5 * own
        target = jnp.where(row < 3, half, jnp.where(row == 3, 1.0, jnp.where(row == 4, norm(half), 0.0)))
        h, m, l = split3(target)
        target = jnp.concatenate([h, h, m, h, l, m], axis=0).astype(BF)
        lefts, rights = [], []
        for n in range(5):
            if n == 0:
                vert, stream, ds, dv = 1, b + 1, 0.0, 0.0
            else:
                code = codes_ref[n - 1, b]
                code = jnp.where(code >= 4, code + 1, code)
                third = lax.div(code, 3)
                ds, dv = third - 1, code - 3 * third - 1
                vert, stream = dv + 1, b + 1 + ds
                ds, dv = ds.astype(F32), dv.astype(F32)
            near = centred(vert, stream, ds, dv)
            half = 0.5 * near
            source = jnp.where(row < 3, -2.0 * half, jnp.where(row == 3, norm(half), jnp.where(row == 4, 1.0, 0.0)))
            h, m, l = split3(source)
            source = jnp.concatenate([h, m, h, l, h, m], axis=0).astype(BF)
            mass = near[6:7]
            weighted = jnp.where(row == 6, 1.0, near) * mass
            dots = near[0:3] * near[3:6]
            dot = mass * (dots[0:1] + dots[1:2] + dots[2:3])
            second = jnp.where(row < 3, weighted * near[7:8], jnp.where(row == 3, dot, 0.0))
            fields = jnp.concatenate([weighted, second], axis=0)
            high = fields.astype(BF)
            low = (fields - high.astype(F32)).astype(BF)
            quarter = lax.dot_general(target, source, TN, preferred_element_type=F32)
            quarter = jnp.maximum(quarter, 1e-30)
            reach = jnp.maximum(1.0 - quarter * lax.rsqrt(quarter), 0.0)
            cube = reach * reach * reach
            cube_high = cube.astype(BF)
            cube_low = (cube - cube_high.astype(F32)).astype(BF)
            left = jnp.concatenate([cube_high, cube_low], axis=1)
            right = jnp.concatenate([jnp.concatenate([high, high], axis=1), jnp.concatenate([low, jnp.zeros_like(low)], axis=1)], axis=0)
            lefts.append(left)
            rights.append(right)
        sums = lax.dot_general(jnp.concatenate(lefts, axis=1), jnp.concatenate(rights, axis=1), NT, preferred_element_type=F32)
        sums = jnp.transpose(sums)
        sums = sums[0:16] + sums[16:32]
        relative = state_ref[pl.ds(7 * b + 6, 1)]
        density = 16.0 * own[6:7]
        place, speed, pressure = own[0:3], own[3:6], own[7:8]
        total, pressure_total, vx = sums[6:7], sums[7:8], sums[11:12]
        dots = speed * (place * total - sums[0:3]) - place * sums[3:6]
        rate = SLOPE * (dots[0:1] + dots[1:2] + dots[2:3] + vx)
        acc = -SLOPE * (pressure * (place * total - sums[0:3]) + place * pressure_total - sums[8:11])
        gravity = jnp.where(row[0:3] == 2, -1.0, 0.0)
        speed = speed + DT * (acc + gravity)
        place = ext_ref[1, b + 1][0:3] + DT * speed
        relative = relative + DT * rate / density
        out_ref[pl.ds(7 * b, 7)] = jnp.concatenate([place, speed, relative], axis=0)
        for c in range(3):
            speed_ref[c, pl.ds(b, 1)] = speed[c : c + 1]
        if next_ref is not None:
            pressure = pressure_of(relative, density)
            next_ref[1, b + 1] = jnp.concatenate([place, speed, own[6:7], pressure], axis=0)

    def several(i, carry):
        for k in range(TRIP):
            one_block(TRIP * i + k)
        if after_trip is not None:
            after_trip(i)
        return carry

    lax.fori_loop(0, blocks // TRIP, several, 0)


def orthonormal_rows(t):
    rank, width = t.shape
    zero = jnp.zeros((width - rank, width), jnp.float32)
    lane = lax.broadcasted_iota(jnp.int32, (rank, width), 1)
    row = lax.broadcasted_iota(jnp.int32, (rank, width), 0)
    unit = jnp.where(lane == row + rank, 1.0, 0.0)
    work = lax.dot_general(t, jnp.concatenate([t, zero], axis=0), NT, precision=HI) + unit
    eight = lax.broadcasted_iota(jnp.int32, (8, width), 0)
    count = rank // 8

    groups = [work[8 * g:8 * g + 8] for g in range(count)]
    for p in range(count):
        live = range(p, count)
        cols = [{g: jnp.broadcast_to(groups[g][:, 8 * p + c:8 * p + c + 1], (8, width)) for g in live} for c in range(8)]
        for k in range(8):
            inv = lax.rsqrt(jnp.broadcast_to(cols[k][p][k:k + 1], (8, width)))
            low = {g: cols[k][g] * inv for g in live}
            pivot_row = jnp.broadcast_to(groups[p][k:k + 1], (8, width)) * inv
            for c in range(k + 1, 8):
                factor = jnp.broadcast_to(low[p][c:c + 1], (8, width))
                for g in live:
                    cols[c][g] = cols[c][g] - low[g] * factor
            groups[p] = jnp.where(eight == k, pivot_row, jnp.where(eight > k, groups[p] - low[p] * pivot_row, groups[p]))
            for g in range(p + 1, count):
                groups[g] = groups[g] - low[g] * pivot_row
    done = jnp.concatenate(groups, axis=0)
    return lax.dot_general(done, jnp.concatenate([zero, t], axis=0), NN, precision=HI)
SIDES = [(ds, dv) for dv in (-1, 0, 1) for ds in (-1, 0, 1) if (ds, dv) != (0, 0)]
LONG = 8
JOIN = 8


def present(ds, dv):
    s, v = lax.axis_index("stream") + ds, lax.axis_index("vert") + dv
    inside_s = jnp.logical_and(s >= 0, s < lax.axis_size("stream"))
    return jnp.logical_and(inside_s, jnp.logical_and(v >= 0, v < lax.axis_size("vert")))


def halo_copy(ext_ref, send_sem, recv_sem, index):
    blocks = ext_ref.shape[1] - 2
    ds, dv = SIDES[index]
    if ds == 0:
        source, target = pl.ds(1, blocks), pl.ds(1, blocks)
    elif ds == 1:
        source, target = pl.ds(blocks, 1), pl.ds(0, 1)
    else:
        source, target = pl.ds(1, 1), pl.ds(blocks + 1, 1)
    source, target = ext_ref.at[1, source], ext_ref.at[1 - dv, target]
    return pltpu.make_async_remote_copy(
        src_ref=source,
        dst_ref=target,
        send_sem=send_sem.at[index],
        recv_sem=recv_sem.at[index],
        device_id=(lax.axis_index("stream") + ds, lax.axis_index("vert") + dv),
        device_id_type=MESH,
    )


def halo_greet(barrier):
    count = 0
    for ds, dv in SIDES:
        here = present(ds, dv)
        count = count + here.astype(jnp.int32)

        @pl.when(here)
        def _():
            device = (lax.axis_index("stream") + ds, lax.axis_index("vert") + dv)
            pl.semaphore_signal(barrier, inc=1, device_id=device, device_id_type=MESH)

    return count


def halo_clear(ext_ref):
    blocks, fields, part = ext_ref.shape[1] - 2, ext_ref.shape[2], ext_ref.shape[3]
    for ds, dv in SIDES:

        @pl.when(jnp.logical_not(present(ds, dv)))
        def _():
            if ds == 0:
                ext_ref[1 + dv, 1 : blocks + 1] = jnp.zeros((blocks, fields, part), F32)
            else:
                ext_ref[1 + dv, 0 if ds < 0 else blocks + 1] = jnp.zeros((fields, part), F32)


FACES = (1, 6)
ENDS = (0, 2, 3, 4, 5, 7)


def halo_start(ext_ref, send_sem, recv_sem, indices):
    for index in indices:

        @pl.when(present(*SIDES[index]))
        def _():
            halo_copy(ext_ref, send_sem, recv_sem, index).start()


def halo_finish(ext_ref, send_sem, recv_sem, indices):
    for index in indices:
        ds, dv = SIDES[index]
        back = SIDES.index((-ds, -dv))

        @pl.when(present(ds, dv))
        def _():
            halo_copy(ext_ref, send_sem, recv_sem, index).wait_send()
            halo_copy(ext_ref, send_sem, recv_sem, back).wait_recv()


def face_copy(ext_ref, send_sem, recv_sem, side, trip):
    dv = SIDES[FACES[side]][1]
    rows = pl.ds(1 + TRIP * trip, TRIP)
    return pltpu.make_async_remote_copy(
        src_ref=ext_ref.at[1, rows],
        dst_ref=ext_ref.at[1 - dv, rows],
        send_sem=send_sem.at[side, trip],
        recv_sem=recv_sem.at[side, trip],
        device_id=(lax.axis_index("stream"), lax.axis_index("vert") + dv),
        device_id_type=MESH,
    )


def face_start(ext_ref, send_sem, recv_sem, trip):
    for side in range(2):

        @pl.when(present(*SIDES[FACES[side]]))
        def _():
            face_copy(ext_ref, send_sem, recv_sem, side, trip).start()


def face_finish(ext_ref, send_sem, recv_sem, trips):
    for side in range(2):

        @pl.when(present(*SIDES[FACES[side]]))
        def _():
            for trip in range(trips):
                face_copy(ext_ref, send_sem, recv_sem, side, trip).wait_send()
                face_copy(ext_ref, send_sem, recv_sem, 1 - side, trip).wait_recv()


def groups():
    stream, vert = lax.axis_index("stream"), lax.axis_index("vert")
    core, z, y = stream % 2, (stream // 2) % LONG, stream // (2 * LONG)
    return (
        (vert * 2 + core, lambda r: (stream - core + r % 2, r // 2)),
        (z, lambda r: (stream + (r - z) * 2, vert)),
        (y, lambda r: (stream + (r - y) * 2 * LONG, vert)),
    )


def group_greet(barrier, me, device):
    for step in range(1, LONG):
        pl.semaphore_signal(barrier, inc=1, device_id=device((me + step) % LONG), device_id_type=MESH)
    return LONG - 1


def group_copies(me, device, source, target, send_sem, recv_sem):
    copies = []
    for step in range(1, LONG):
        other = (me + step) % LONG
        copies.append(
            pltpu.make_async_remote_copy(
                src_ref=source(other),
                dst_ref=target(step),
                send_sem=send_sem.at[step],
                recv_sem=recv_sem.at[step],
                device_id=device(other),
                device_id_type=MESH,
            )
        )
    return copies


def start(copies):
    for copy in copies:
        copy.start()


def finish(copies):
    for copy in copies:
        copy.wait()


def total(own, slots_ref):
    for step in range(1, LONG):
        own = own + slots_ref[step]
    return own


def shard_of(index, size):
    return pl.ds(pl.multiple_of(index * size, size), size)


def rounded(speed_ref):
    return [speed_ref[c].astype(BF).astype(F32) for c in range(3)]


def plane_products(planes, others, products_ref, s):
    acc = None
    for plane, other in zip(planes, others):
        term = plane * other
        acc = term if acc is None else acc + term
    blocks = acc.shape[0]
    folded = acc[0:8]
    for g in range(1, blocks // 8):
        folded = folded + acc[8 * g : 8 * g + 8]
    products_ref[pl.ds(pl.multiple_of(8 * s, 8), 8)] = folded


def inner_products(newest, past_ref, products_ref):
    past = past_ref.shape[1]

    def several(i, carry):
        for k in range(3):
            s = 3 * i + k
            plane_products(newest, [past_ref[c, s].astype(F32) for c in range(3)], products_ref, s)
        return carry

    lax.fori_loop(0, past // 3, several, 0)


def product_row(products_ref):
    snaps = products_ref.shape[0] // 8
    sums = products_ref[pl.ds(0, snaps, stride=8)]
    for q in range(1, 8):
        sums = sums + products_ref[pl.ds(q, snaps, stride=8)]
    return lax.dot_general(jnp.ones((8, sums.shape[1]), F32), sums, NT, precision=HI)


def past_gram(past_ref, gram_ref):
    past, blocks = past_ref.shape[1], past_ref.shape[2]
    gram_ref[...] = jnp.zeros(gram_ref.shape, F32)
    sums = jnp.zeros((past, past), F32)
    for c in range(past_ref.shape[0]):
        planes = jnp.swapaxes(past_ref[c], 0, 1)
        for b in range(0, blocks, JOIN):
            joined = jnp.concatenate([planes[b + k] for k in range(JOIN)], axis=1)
            sums = sums + lax.dot_general(joined, joined, NT, preferred_element_type=F32)
    gram_ref[0:past, 0:past] = sums


def modes(gram_ref, rows, basis_ref, speed_1, speed_2, past, out_ref, full_ref, weights):
    width = gram_ref.shape[0]
    across = jnp.transpose(jnp.concatenate([rows, jnp.zeros((width - rows.shape[0], width), F32)], axis=0))
    lane = lax.broadcasted_iota(jnp.int32, (width, width), 1)
    row = lax.broadcasted_iota(jnp.int32, (width, width), 0)
    full = gram_ref[...]
    for k in range(2):
        place = width - 2 + k
        full = jnp.where(lane == place, jnp.broadcast_to(across[:, k : k + 1], full.shape), full)
        full = jnp.where(row == place, jnp.broadcast_to(rows[k : k + 1], full.shape), full)
    full_ref[...] = full

    def times_gram(t):
        return lax.dot_general(t, full_ref[...], NN, precision=HI)

    def half(i, t):
        t = orthonormal_rows(t)
        again = jnp.logical_and(i % 2 == 1, i < 2 * POD_ITERS - 1)
        return lax.cond(again, times_gram, lambda t: t, t)

    t = lax.fori_loop(0, 2 * POD_ITERS, half, times_gram(basis_ref[...]))
    last = jnp.broadcast_to(t[:, width - 1 : width], t.shape)
    weights[...] = lax.dot_general(t, last, TN, precision=HI)
    snaps = past.shape[1]

    def several(i, sums):
        for k in range(3):
            s = 3 * i + k
            weight = jnp.broadcast_to(weights[pl.ds(s, 1)], sums[0].shape)
            sums = tuple(total + past[c, s].astype(F32) * weight for c, total in enumerate(sums))
        return sums

    zero = jnp.zeros(speed_1.shape[1:], F32)
    sums = lax.fori_loop(0, snaps // 3, several, (zero, zero, zero))
    for k, speed_ref in enumerate((speed_1, speed_2)):
        weight = jnp.broadcast_to(weights[width - 2 + k : width - 1 + k], zero.shape)
        sums = [total + plane * weight for total, plane in zip(sums, rounded(speed_ref))]
    for c in range(3):
        out_ref[pl.ds(c, zero.shape[0], stride=3)] = sums[c]


def flow_kernel(
    codes_ref, state_ref, flags_ref, start_ref, past_hbm,
    out_ref, filtered_ref, speed_1, speed_2, gram_out, basis_ref, full, weights,
    gram_ref, ext_1, ext_2, middle, past, products, rows, piece, near_slots, long_slots, row_slots,
    past_sem, face_send, face_recv, send_1, recv_1, send_2, recv_2, near_send, near_recv, long_send, long_recv,
    all_send, all_recv, row_send, row_recv,
):
    near, z, y = groups()
    blocks, part = flags_ref.shape
    snaps = gram_ref.shape[0]
    size = snaps // LONG
    load = pltpu.make_async_copy(past_hbm, past, past_sem)
    load.start()
    barrier = pltpu.get_barrier_semaphore()
    count = halo_greet(barrier)
    for group in (near, z, y):
        count = count + group_greet(barrier, *group)
    density = 1.0 + SEDIMENT_EXTRA * flags_ref[...].astype(F32)
    mass = density * VOLUME
    pressure = pressure_of(state_ref[pl.ds(6, blocks, stride=7)], density)
    for b in range(blocks):
        ext_1[1, b + 1, 0:6] = state_ref[7 * b : 7 * b + 6]
        ext_1[1, b + 1, 6:7] = mass[b : b + 1]
        ext_1[1, b + 1, 7:8] = pressure[b : b + 1]
    halo_clear(ext_1)
    halo_clear(ext_2)
    products[pl.ds(8 * (snaps - 2), 16)] = jnp.zeros((16, part), F32)
    load.wait()
    past_gram(past, gram_ref)
    pl.semaphore_wait(barrier, count)

    halo_start(ext_1, send_1, recv_1, FACES + ENDS)
    scatter = group_copies(
        *near, lambda other: gram_ref.at[shard_of(other, size)], lambda step: near_slots.at[step], near_send, near_recv
    )
    start(scatter)
    basis_ref[...] = start_ref[...]

    @pl.loop(0, 2)
    def _(i):
        basis_ref[...] = orthonormal_rows(basis_ref[...])

    finish(scatter)
    piece[0] = total(gram_ref[shard_of(near[0], size)], near_slots)
    over_z = group_copies(*z, lambda other: piece.at[0], lambda step: long_slots.at[0, step], long_send.at[0], long_recv.at[0])
    start(over_z)
    halo_finish(ext_1, send_1, recv_1, FACES + ENDS)

    def send_previous(i):
        @pl.when(i > 0)
        def _():
            face_start(ext_2, face_send, face_recv, i - 1)

    forces(codes_ref, ext_1, state_ref, middle, speed_1, ext_2, send_previous)

    trips = blocks // TRIP
    finish(over_z)
    piece[1] = total(piece[0], long_slots.at[0])
    face_start(ext_2, face_send, face_recv, trips - 1)
    halo_start(ext_2, send_2, recv_2, ENDS)
    over_y = group_copies(*y, lambda other: piece.at[1], lambda step: long_slots.at[1, step], long_send.at[1], long_recv.at[1])
    start(over_y)
    first = rounded(speed_1)
    inner_products(first, past, products)
    plane_products(first, first, products, snaps - 2)
    rows[0] = product_row(products)
    halo_finish(ext_2, send_2, recv_2, ENDS)
    face_finish(ext_2, face_send, face_recv, trips)
    forces(codes_ref, ext_2, middle, out_ref, speed_2)

    finish(over_y)
    whole = total(piece[1], long_slots.at[1])
    piece[2] = whole
    gram_out[shard_of(near[0], size)] = whole
    second = rounded(speed_2)
    inner_products(second, past, products)
    plane_products(second, rounded(speed_1), products, snaps - 2)
    plane_products(second, second, products, snaps - 1)
    eight = lax.broadcasted_iota(jnp.int32, (8, snaps), 0)
    value = jnp.where(eight == 0, rows[0], product_row(products))
    gathers = group_copies(*near, lambda other: piece.at[2], lambda step: gram_out.at[shard_of(near[0], size)], all_send, all_recv)
    for stage, group in enumerate((z, y, near)):
        rows[1 + stage] = value
        copies = group_copies(
            *group, lambda other: rows.at[1 + stage], lambda step: row_slots.at[stage, step],
            row_send.at[stage], row_recv.at[stage],
        )
        start(copies)
        if stage == 0:
            start(gathers)
        finish(copies)
        value = total(value, row_slots.at[stage])
    rows[4] = value
    finish(gathers)
    modes(gram_out, rows[4], basis_ref, speed_1, speed_2, past, filtered_ref, full, weights)


def flow(codes, state, flags, start_rows, past):
    blocks, part = flags.shape
    rank, snaps = start_rows.shape
    shard = snaps // LONG
    dma = pltpu.SemaphoreType.DMA
    ext = pltpu.VMEM((3, blocks + 2, 8, part), F32)
    shapes = [state.shape, (3 * blocks, part)]
    square, speed = pltpu.VMEM((snaps, snaps), F32), pltpu.VMEM((3, blocks, part), F32)
    return pl.pallas_call(
        flow_kernel,
        out_shape=[jax.ShapeDtypeStruct(shape, F32) for shape in shapes],
        in_specs=[pl.BlockSpec(memory_space=pltpu.SMEM), VM, VM, VM, pl.BlockSpec(memory_space=pl.ANY)],
        out_specs=[VM] * len(shapes),
        scratch_shapes=[
            speed, speed, square, pltpu.VMEM((rank, snaps), F32), square, square, square,
            ext, ext,
            pltpu.VMEM(state.shape, F32),
            pltpu.VMEM(past.shape, BF),
            pltpu.VMEM((8 * snaps, part), F32),
            pltpu.VMEM((5, 8, snaps), F32),
            pltpu.VMEM((3, shard, snaps), F32),
            pltpu.VMEM((LONG, shard, snaps), F32),
            pltpu.VMEM((2, LONG, shard, snaps), F32),
            pltpu.VMEM((3, LONG, 8, snaps), F32),
            dma, dma((2, blocks // TRIP)), dma((2, blocks // TRIP)), dma((8,)), dma((8,)), dma((8,)), dma((8,)), dma((LONG,)), dma((LONG,)), dma((2, LONG)), dma((2, LONG)),
            dma((LONG,)), dma((LONG,)), dma((3, LONG)), dma((3, LONG)),
        ],
        compiler_params=pltpu.CompilerParams(collective_id=0, has_side_effects=True),
        name="flow",
    )(codes, state, flags, start_rows, past)


def deliver_kernel(state_ref, filtered_ref, state_out, filtered_out):
    state_out[...] = state_ref[...]
    filtered_out[...] = filtered_ref[...]


def deliver(*arrays):
    return pl.pallas_call(
        deliver_kernel,
        out_shape=[jax.ShapeDtypeStruct(array.shape, F32) for array in arrays],
        in_specs=[VM, VM],
        out_specs=[VM, VM],
        name="deliver",
    )(*arrays)


def body(particles, phase_flags, neighbours, history, basis_start):
    blocks, _, fields, part = particles.shape
    state = particles.reshape(blocks * fields, part)
    past = jnp.transpose(history[:, 0], (1, 2, 0, 3))
    state, filtered = flow(
        neighbours[:, 0].T, state, phase_flags[:, 0], basis_start.T, past
    )
    state, filtered = deliver(state, filtered)
    return (state.reshape(particles.shape), filtered.reshape(blocks, 1, 3, part))


def solution(mesh):
    in_specs = (
        P("stream", "vert", None, None),
        P("stream", "vert", None),
        P("stream", "vert", None),
        P("stream", "vert", None, None, None),
        P(),
    )
    out_specs = (P("stream", "vert", None, None), P("stream", "vert", None, None))
    return jax.shard_map(body, mesh=mesh, in_specs=in_specs, out_specs=out_specs, check_vma=False)
```

```python
import functools
import math

import jax
import jax.numpy as jnp
from jax import lax
from jax.experimental import pallas as pl
from jax.experimental.pallas import tpu as pltpu
from jax.sharding import PartitionSpec as P

POD_ITERS = 4
VOLUME = 1.0 / 16.0
STIFFNESS = 100.0 / 7.0
SLOPE = -5.0 * 21.0 / (16.0 * math.pi)
DT = 0.02
SEDIMENT_EXTRA = 1.65

HI = lax.Precision.HIGHEST
NT = (((1,), (1,)), ((), ()))
NN = (((1,), (0,)), ((), ()))
TN = (((0,), (0,)), ((), ()))
BF = jnp.bfloat16
F32 = jnp.float32
MESH = pl.DeviceIdType.MESH
VM = pl.BlockSpec(memory_space=pltpu.VMEM)

TRIP = 8


def pressure_of(relative, density):
    power = relative * relative
    power = power * power * power * relative
    return STIFFNESS * (power - 1.0) / (density * relative * relative)


def split3(x):
    a = x.astype(BF).astype(F32)
    b = (x - a).astype(BF).astype(F32)
    return a, b, x - a - b


def forces(codes_ref, ext_ref, state_ref, out_ref, speed_ref, next_ref=None, after_trip=None):
    blocks, part = ext_ref.shape[1] - 2, ext_ref.shape[3]
    row = lax.broadcasted_iota(jnp.int32, (8, part), 0)

    def centred(vert, stream, ds, dv):
        field = ext_ref[vert, stream]
        shift = jnp.where(row == 0, 2.0 * ds - 1.0, jnp.where(row == 1, -1.0, jnp.where(row == 2, 2.0 * dv - 1.0, 0.0)))
        return field + shift

    def norm(half):
        square = half * half
        return square[0:1] + square[1:2] + square[2:3]

    def one_block(b):
        own = centred(1, b + 1, 0.0, 0.0)
        half = 0.5 * own
        target = jnp.where(row < 3, half, jnp.where(row == 3, 1.0, jnp.where(row == 4, norm(half), 0.0)))
        h, m, l = split3(target)
        target = jnp.concatenate([h, h, m, h, l, m], axis=0).astype(BF)
        lefts, rights = [], []
        for n in range(5):
            if n == 0:
                vert, stream, ds, dv = 1, b + 1, 0.0, 0.0
            else:
                code = codes_ref[n - 1, b]
                code = jnp.where(code >= 4, code + 1, code)
                third = lax.div(code, 3)
                ds, dv = third - 1, code - 3 * third - 1
                vert, stream = dv + 1, b + 1 + ds
                ds, dv = ds.astype(F32), dv.astype(F32)
            near = centred(vert, stream, ds, dv)
            half = 0.5 * near
            source = jnp.where(row < 3, -2.0 * half, jnp.where(row == 3, norm(half), jnp.where(row == 4, 1.0, 0.0)))
            h, m, l = split3(source)
            source = jnp.concatenate([h, m, h, l, h, m], axis=0).astype(BF)
            mass = near[6:7]
            weighted = jnp.where(row == 6, 1.0, near) * mass
            dots = near[0:3] * near[3:6]
            dot = mass * (dots[0:1] + dots[1:2] + dots[2:3])
            second = jnp.where(row < 3, weighted * near[7:8], jnp.where(row == 3, dot, 0.0))
            fields = jnp.concatenate([weighted, second], axis=0)
            high = fields.astype(BF)
            low = (fields - high.astype(F32)).astype(BF)
            quarter = lax.dot_general(target, source, TN, preferred_element_type=F32)
            quarter = jnp.maximum(quarter, 1e-30)
            reach = jnp.maximum(1.0 - quarter * lax.rsqrt(quarter), 0.0)
            cube = reach * reach * reach
            cube_high = cube.astype(BF)
            cube_low = (cube - cube_high.astype(F32)).astype(BF)
            left = jnp.concatenate([cube_high, cube_low], axis=1)
            right = jnp.concatenate([jnp.concatenate([high, high], axis=1), jnp.concatenate([low, jnp.zeros_like(low)], axis=1)], axis=0)
            lefts.append(left)
            rights.append(right)
        sums = lax.dot_general(jnp.concatenate(lefts, axis=1), jnp.concatenate(rights, axis=1), NT, preferred_element_type=F32)
        sums = jnp.transpose(sums)
        sums = sums[0:16] + sums[16:32]
        relative = state_ref[pl.ds(7 * b + 6, 1)]
        density = 16.0 * own[6:7]
        place, speed, pressure = own[0:3], own[3:6], own[7:8]
        total, pressure_total, vx = sums[6:7], sums[7:8], sums[11:12]
        dots = speed * (place * total - sums[0:3]) - place * sums[3:6]
        rate = SLOPE * (dots[0:1] + dots[1:2] + dots[2:3] + vx)
        acc = -SLOPE * (pressure * (place * total - sums[0:3]) + place * pressure_total - sums[8:11])
        gravity = jnp.where(row[0:3] == 2, -1.0, 0.0)
        speed = speed + DT * (acc + gravity)
        place = ext_ref[1, b + 1][0:3] + DT * speed
        relative = relative + DT * rate / density
        out_ref[pl.ds(7 * b, 7)] = jnp.concatenate([place, speed, relative], axis=0)
        for c in range(3):
            speed_ref[c, pl.ds(b, 1)] = speed[c : c + 1]
        if next_ref is not None:
            pressure = pressure_of(relative, density)
            next_ref[1, b + 1] = jnp.concatenate([place, speed, own[6:7], pressure], axis=0)

    def several(i, carry):
        for k in range(TRIP):
            one_block(TRIP * i + k)
        if after_trip is not None:
            after_trip(i)
        return carry

    lax.fori_loop(0, blocks // TRIP, several, 0)


def orthonormal_rows(t):
    rank, width = t.shape
    zero = jnp.zeros((width - rank, width), jnp.float32)
    lane = lax.broadcasted_iota(jnp.int32, (rank, width), 1)
    row = lax.broadcasted_iota(jnp.int32, (rank, width), 0)
    unit = jnp.where(lane == row + rank, 1.0, 0.0)
    work = lax.dot_general(t, jnp.concatenate([t, zero], axis=0), NT, precision=HI) + unit
    eight = lax.broadcasted_iota(jnp.int32, (8, width), 0)
    count = rank // 8

    groups = [work[8 * g:8 * g + 8] for g in range(count)]
    for p in range(count):
        live = range(p, count)
        cols = [{g: jnp.broadcast_to(groups[g][:, 8 * p + c:8 * p + c + 1], (8, width)) for g in live} for c in range(8)]
        for k in range(8):
            inv = lax.rsqrt(jnp.broadcast_to(cols[k][p][k:k + 1], (8, width)))
            low = {g: cols[k][g] * inv for g in live}
            pivot_row = jnp.broadcast_to(groups[p][k:k + 1], (8, width)) * inv
            for c in range(k + 1, 8):
                factor = jnp.broadcast_to(low[p][c:c + 1], (8, width))
                for g in live:
                    cols[c][g] = cols[c][g] - low[g] * factor
            groups[p] = jnp.where(eight == k, pivot_row, jnp.where(eight > k, groups[p] - low[p] * pivot_row, groups[p]))
            for g in range(p + 1, count):
                groups[g] = groups[g] - low[g] * pivot_row
    done = jnp.concatenate(groups, axis=0)
    return lax.dot_general(done, jnp.concatenate([zero, t], axis=0), NN, precision=HI)
SIDES = [(ds, dv) for dv in (-1, 0, 1) for ds in (-1, 0, 1) if (ds, dv) != (0, 0)]
LONG = 8
JOIN = 8


def present(ds, dv):
    s, v = lax.axis_index("stream") + ds, lax.axis_index("vert") + dv
    inside_s = jnp.logical_and(s >= 0, s < lax.axis_size("stream"))
    return jnp.logical_and(inside_s, jnp.logical_and(v >= 0, v < lax.axis_size("vert")))


def halo_copy(ext_ref, send_sem, recv_sem, index):
    blocks = ext_ref.shape[1] - 2
    ds, dv = SIDES[index]
    if ds == 0:
        source, target = pl.ds(1, blocks), pl.ds(1, blocks)
    elif ds == 1:
        source, target = pl.ds(blocks, 1), pl.ds(0, 1)
    else:
        source, target = pl.ds(1, 1), pl.ds(blocks + 1, 1)
    source, target = ext_ref.at[1, source], ext_ref.at[1 - dv, target]
    return pltpu.make_async_remote_copy(
        src_ref=source,
        dst_ref=target,
        send_sem=send_sem.at[index],
        recv_sem=recv_sem.at[index],
        device_id=(lax.axis_index("stream") + ds, lax.axis_index("vert") + dv),
        device_id_type=MESH,
    )


def halo_greet(barrier):
    count = 0
    for ds, dv in SIDES:
        here = present(ds, dv)
        count = count + here.astype(jnp.int32)

        @pl.when(here)
        def _():
            device = (lax.axis_index("stream") + ds, lax.axis_index("vert") + dv)
            pl.semaphore_signal(barrier, inc=1, device_id=device, device_id_type=MESH)

    return count


def halo_clear(ext_ref):
    blocks, fields, part = ext_ref.shape[1] - 2, ext_ref.shape[2], ext_ref.shape[3]
    for ds, dv in SIDES:

        @pl.when(jnp.logical_not(present(ds, dv)))
        def _():
            if ds == 0:
                ext_ref[1 + dv, 1 : blocks + 1] = jnp.zeros((blocks, fields, part), F32)
            else:
                ext_ref[1 + dv, 0 if ds < 0 else blocks + 1] = jnp.zeros((fields, part), F32)


FACES = (1, 6)
ENDS = (0, 2, 3, 4, 5, 7)


def halo_start(ext_ref, send_sem, recv_sem, indices):
    for index in indices:

        @pl.when(present(*SIDES[index]))
        def _():
            halo_copy(ext_ref, send_sem, recv_sem, index).start()


def halo_finish(ext_ref, send_sem, recv_sem, indices):
    for index in indices:
        ds, dv = SIDES[index]
        back = SIDES.index((-ds, -dv))

        @pl.when(present(ds, dv))
        def _():
            halo_copy(ext_ref, send_sem, recv_sem, index).wait_send()
            halo_copy(ext_ref, send_sem, recv_sem, back).wait_recv()


def face_copy(ext_ref, send_sem, recv_sem, side, trip):
    dv = SIDES[FACES[side]][1]
    rows = pl.ds(1 + TRIP * trip, TRIP)
    return pltpu.make_async_remote_copy(
        src_ref=ext_ref.at[1, rows],
        dst_ref=ext_ref.at[1 - dv, rows],
        send_sem=send_sem.at[side, trip],
        recv_sem=recv_sem.at[side, trip],
        device_id=(lax.axis_index("stream"), lax.axis_index("vert") + dv),
        device_id_type=MESH,
    )


def face_start(ext_ref, send_sem, recv_sem, trip):
    for side in range(2):

        @pl.when(present(*SIDES[FACES[side]]))
        def _():
            face_copy(ext_ref, send_sem, recv_sem, side, trip).start()


def face_finish(ext_ref, send_sem, recv_sem, trips):
    for side in range(2):

        @pl.when(present(*SIDES[FACES[side]]))
        def _():
            for trip in range(trips):
                face_copy(ext_ref, send_sem, recv_sem, side, trip).wait_send()
                face_copy(ext_ref, send_sem, recv_sem, 1 - side, trip).wait_recv()


def groups():
    stream, vert = lax.axis_index("stream"), lax.axis_index("vert")
    core, z, y = stream % 2, (stream // 2) % LONG, stream // (2 * LONG)
    return (
        (vert * 2 + core, lambda r: (stream - core + r % 2, r // 2)),
        (z, lambda r: (stream + (r - z) * 2, vert)),
        (y, lambda r: (stream + (r - y) * 2 * LONG, vert)),
    )


def group_greet(barrier, me, device):
    for step in range(1, LONG):
        pl.semaphore_signal(barrier, inc=1, device_id=device((me + step) % LONG), device_id_type=MESH)
    return LONG - 1


def group_copies(me, device, source, target, send_sem, recv_sem):
    copies = []
    for step in range(1, LONG):
        other = (me + step) % LONG
        copies.append(
            pltpu.make_async_remote_copy(
                src_ref=source(other),
                dst_ref=target(step),
                send_sem=send_sem.at[step],
                recv_sem=recv_sem.at[step],
                device_id=device(other),
                device_id_type=MESH,
            )
        )
    return copies


def start(copies):
    for copy in copies:
        copy.start()


def finish(copies):
    for copy in copies:
        copy.wait()


def total(own, slots_ref):
    for step in range(1, LONG):
        own = own + slots_ref[step]
    return own


def shard_of(index, size):
    return pl.ds(pl.multiple_of(index * size, size), size)


def rounded(speed_ref):
    return [speed_ref[c].astype(BF).astype(F32) for c in range(3)]


def plane_products(planes, others, products_ref, s):
    acc = None
    for plane, other in zip(planes, others):
        term = plane * other
        acc = term if acc is None else acc + term
    blocks = acc.shape[0]
    folded = acc[0:8]
    for g in range(1, blocks // 8):
        folded = folded + acc[8 * g : 8 * g + 8]
    products_ref[pl.ds(pl.multiple_of(8 * s, 8), 8)] = folded


def inner_products(newest, past_ref, products_ref):
    past = past_ref.shape[1]

    def several(i, carry):
        for k in range(3):
            s = 3 * i + k
            plane_products(newest, [past_ref[c, s].astype(F32) for c in range(3)], products_ref, s)
        return carry

    lax.fori_loop(0, past // 3, several, 0)


def product_row(products_ref):
    snaps = products_ref.shape[0] // 8
    sums = products_ref[pl.ds(0, snaps, stride=8)]
    for q in range(1, 8):
        sums = sums + products_ref[pl.ds(q, snaps, stride=8)]
    return lax.dot_general(jnp.ones((8, sums.shape[1]), F32), sums, NT, precision=HI)


def past_gram(past_ref, gram_ref):
    past, blocks = past_ref.shape[1], past_ref.shape[2]
    gram_ref[...] = jnp.zeros(gram_ref.shape, F32)
    sums = jnp.zeros((past, past), F32)
    for c in range(past_ref.shape[0]):
        planes = jnp.swapaxes(past_ref[c], 0, 1)
        for b in range(0, blocks, JOIN):
            joined = jnp.concatenate([planes[b + k] for k in range(JOIN)], axis=1)
            sums = sums + lax.dot_general(joined, joined, NT, preferred_element_type=F32)
    gram_ref[0:past, 0:past] = sums


def modes(gram_ref, rows, basis_ref, speed_1, speed_2, past, out_ref, full_ref, weights):
    width = gram_ref.shape[0]
    across = jnp.transpose(jnp.concatenate([rows, jnp.zeros((width - rows.shape[0], width), F32)], axis=0))
    lane = lax.broadcasted_iota(jnp.int32, (width, width), 1)
    row = lax.broadcasted_iota(jnp.int32, (width, width), 0)
    full = gram_ref[...]
    for k in range(2):
        place = width - 2 + k
        full = jnp.where(lane == place, jnp.broadcast_to(across[:, k : k + 1], full.shape), full)
        full = jnp.where(row == place, jnp.broadcast_to(rows[k : k + 1], full.shape), full)
    full_ref[...] = full

    def times_gram(t):
        return lax.dot_general(t, full_ref[...], NN, precision=HI)

    def half(i, t):
        t = orthonormal_rows(t)
        again = jnp.logical_and(i % 2 == 1, i < 2 * POD_ITERS - 1)
        return lax.cond(again, times_gram, lambda t: t, t)

    t = lax.fori_loop(0, 2 * POD_ITERS, half, times_gram(basis_ref[...]))
    last = jnp.broadcast_to(t[:, width - 1 : width], t.shape)
    weights[...] = lax.dot_general(t, last, TN, precision=HI)
    snaps = past.shape[1]

    def several(i, sums):
        for k in range(3):
            s = 3 * i + k
            weight = jnp.broadcast_to(weights[pl.ds(s, 1)], sums[0].shape)
            sums = tuple(total + past[c, s].astype(F32) * weight for c, total in enumerate(sums))
        return sums

    zero = jnp.zeros(speed_1.shape[1:], F32)
    sums = lax.fori_loop(0, snaps // 3, several, (zero, zero, zero))
    for k, speed_ref in enumerate((speed_1, speed_2)):
        weight = jnp.broadcast_to(weights[width - 2 + k : width - 1 + k], zero.shape)
        sums = [total + plane * weight for total, plane in zip(sums, rounded(speed_ref))]
    for c in range(3):
        out_ref[pl.ds(c, zero.shape[0], stride=3)] = sums[c]


def flow_kernel(
    codes_ref, state_ref, flags_ref, start_ref, past_hbm,
    out_ref, filtered_ref, speed_1, speed_2, gram_out, basis_ref, full, weights,
    gram_ref, ext_1, ext_2, middle, past, products, rows, piece, near_slots, long_slots, row_slots,
    past_sem, face_send, face_recv, send_1, recv_1, send_2, recv_2, near_send, near_recv, long_send, long_recv,
    all_send, all_recv, row_send, row_recv,
):
    near, z, y = groups()
    blocks, part = flags_ref.shape
    snaps = gram_ref.shape[0]
    size = snaps // LONG
    load = pltpu.make_async_copy(past_hbm, past, past_sem)
    load.start()
    barrier = pltpu.get_barrier_semaphore()
    count = halo_greet(barrier)
    for group in (near, z, y):
        count = count + group_greet(barrier, *group)
    density = 1.0 + SEDIMENT_EXTRA * flags_ref[...].astype(F32)
    mass = density * VOLUME
    pressure = pressure_of(state_ref[pl.ds(6, blocks, stride=7)], density)
    for b in range(blocks):
        ext_1[1, b + 1, 0:6] = state_ref[7 * b : 7 * b + 6]
        ext_1[1, b + 1, 6:7] = mass[b : b + 1]
        ext_1[1, b + 1, 7:8] = pressure[b : b + 1]
    halo_clear(ext_1)
    halo_clear(ext_2)
    products[pl.ds(8 * (snaps - 2), 16)] = jnp.zeros((16, part), F32)
    load.wait()
    past_gram(past, gram_ref)
    pl.semaphore_wait(barrier, count)

    halo_start(ext_1, send_1, recv_1, FACES + ENDS)
    scatter = group_copies(
        *near, lambda other: gram_ref.at[shard_of(other, size)], lambda step: near_slots.at[step], near_send, near_recv
    )
    start(scatter)
    basis_ref[...] = start_ref[...]

    @pl.loop(0, 2)
    def _(i):
        basis_ref[...] = orthonormal_rows(basis_ref[...])

    finish(scatter)
    piece[0] = total(gram_ref[shard_of(near[0], size)], near_slots)
    over_z = group_copies(*z, lambda other: piece.at[0], lambda step: long_slots.at[0, step], long_send.at[0], long_recv.at[0])
    start(over_z)
    halo_finish(ext_1, send_1, recv_1, FACES + ENDS)

    def send_previous(i):
        @pl.when(i > 0)
        def _():
            face_start(ext_2, face_send, face_recv, i - 1)

    forces(codes_ref, ext_1, state_ref, middle, speed_1, ext_2, send_previous)

    trips = blocks // TRIP
    finish(over_z)
    piece[1] = total(piece[0], long_slots.at[0])
    face_start(ext_2, face_send, face_recv, trips - 1)
    halo_start(ext_2, send_2, recv_2, ENDS)
    over_y = group_copies(*y, lambda other: piece.at[1], lambda step: long_slots.at[1, step], long_send.at[1], long_recv.at[1])
    start(over_y)
    first = rounded(speed_1)
    inner_products(first, past, products)
    plane_products(first, first, products, snaps - 2)
    rows[0] = product_row(products)
    halo_finish(ext_2, send_2, recv_2, ENDS)
    face_finish(ext_2, face_send, face_recv, trips)
    forces(codes_ref, ext_2, middle, out_ref, speed_2)

    finish(over_y)
    whole = total(piece[1], long_slots.at[1])
    piece[2] = whole
    gram_out[shard_of(near[0], size)] = whole
    second = rounded(speed_2)
    inner_products(second, past, products)
    plane_products(second, rounded(speed_1), products, snaps - 2)
    plane_products(second, second, products, snaps - 1)
    eight = lax.broadcasted_iota(jnp.int32, (8, snaps), 0)
    value = jnp.where(eight == 0, rows[0], product_row(products))[0:2]
    pair = pl.ds(0, 2)
    gathers = group_copies(*near, lambda other: piece.at[2], lambda step: gram_out.at[shard_of(near[0], size)], all_send, all_recv)
    for stage, group in enumerate((z, y, near)):
        rows[1 + stage, 0:2] = value
        copies = group_copies(
            *group, lambda other: rows.at[1 + stage, pair], lambda step: row_slots.at[stage, step, pair],
            row_send.at[stage], row_recv.at[stage],
        )
        start(copies)
        if stage == 0:
            start(gathers)
        finish(copies)
        for step in range(1, LONG):
            value = value + row_slots[stage, step, 0:2]
    rows[4] = jnp.zeros(rows.shape[1:], F32)
    rows[4, 0:2] = value
    finish(gathers)
    modes(gram_out, rows[4], basis_ref, speed_1, speed_2, past, filtered_ref, full, weights)


def flow(codes, state, flags, start_rows, past):
    blocks, part = flags.shape
    rank, snaps = start_rows.shape
    shard = snaps // LONG
    dma = pltpu.SemaphoreType.DMA
    ext = pltpu.VMEM((3, blocks + 2, 8, part), F32)
    shapes = [state.shape, (3 * blocks, part)]
    square, speed = pltpu.VMEM((snaps, snaps), F32), pltpu.VMEM((3, blocks, part), F32)
    return pl.pallas_call(
        flow_kernel,
        out_shape=[jax.ShapeDtypeStruct(shape, F32) for shape in shapes],
        in_specs=[pl.BlockSpec(memory_space=pltpu.SMEM), VM, VM, VM, pl.BlockSpec(memory_space=pl.ANY)],
        out_specs=[VM] * len(shapes),
        scratch_shapes=[
            speed, speed, square, pltpu.VMEM((rank, snaps), F32), square, square, square,
            ext, ext,
            pltpu.VMEM(state.shape, F32),
            pltpu.VMEM(past.shape, BF),
            pltpu.VMEM((8 * snaps, part), F32),
            pltpu.VMEM((5, 8, snaps), F32),
            pltpu.VMEM((3, shard, snaps), F32),
            pltpu.VMEM((LONG, shard, snaps), F32),
            pltpu.VMEM((2, LONG, shard, snaps), F32),
            pltpu.VMEM((3, LONG, 8, snaps), F32),
            dma, dma((2, blocks // TRIP)), dma((2, blocks // TRIP)), dma((8,)), dma((8,)), dma((8,)), dma((8,)), dma((LONG,)), dma((LONG,)), dma((2, LONG)), dma((2, LONG)),
            dma((LONG,)), dma((LONG,)), dma((3, LONG)), dma((3, LONG)),
        ],
        compiler_params=pltpu.CompilerParams(collective_id=0, has_side_effects=True),
        name="flow",
    )(codes, state, flags, start_rows, past)


def deliver_kernel(state_ref, filtered_ref, state_out, filtered_out):
    state_out[...] = state_ref[...]
    filtered_out[...] = filtered_ref[...]


def deliver(*arrays):
    return pl.pallas_call(
        deliver_kernel,
        out_shape=[jax.ShapeDtypeStruct(array.shape, F32) for array in arrays],
        in_specs=[VM, VM],
        out_specs=[VM, VM],
        name="deliver",
    )(*arrays)


def body(particles, phase_flags, neighbours, history, basis_start):
    blocks, _, fields, part = particles.shape
    state = particles.reshape(blocks * fields, part)
    past = jnp.transpose(history[:, 0], (1, 2, 0, 3))
    state, filtered = flow(
        neighbours[:, 0].T, state, phase_flags[:, 0], basis_start.T, past
    )
    state, filtered = deliver(state, filtered)
    return (state.reshape(particles.shape), filtered.reshape(blocks, 1, 3, part))


def solution(mesh):
    in_specs = (
        P("stream", "vert", None, None),
        P("stream", "vert", None),
        P("stream", "vert", None),
        P("stream", "vert", None, None, None),
        P(),
    )
    out_specs = (P("stream", "vert", None, None), P("stream", "vert", None, None))
    return jax.shard_map(body, mesh=mesh, in_specs=in_specs, out_specs=out_specs, check_vma=False)
```
